512 devices in a mesh: gx: 32 (over z, x), gy: 16 (over y, core).
Axes of the slice: x: 4, y: 8, z: 8, core: 2. Of those that a mesh axis runs over, the one named last changes fastest.
Arguments:
- state: float32 [5, 16, 256, 2048], P(None, None, 'gx', 'gy'), may hold values from -3 to 60, as said below
- counts: int32 [5, 1, 32, 256], P(None, None, 'gx', 'gy'), may hold values from 1 to 15, as said below
- aggregator: int32 [32], P('gx'), may hold values from 0 to 15
Outputs:
- advanced: float32 [5, 8, 256, 2048], P(None, None, 'gx', 'gy')
- snapshot: float32 [32, 16, 10240], P('gx', 'gy')
The draws below stay inside these ranges and needn't reach their ends.
Inputs may be any that keep to these rules, and one draw needn't show every extreme that they name: state has positive density and pressure. `counts`: the blocks of one x tile and one y tile keep at most 80 * (13) and at least 80 * (3) coefficients in all, and some y tile of every x tile keeps exactly the most; the blocks of one x tile keep exactly 10240 together.
All inputs are finite; a program needn't handle non-finite values.
Results may differ from the reference program's by a relative error of at most 0.0003.
Values sent between devices are 32-bit elements; how exact they have to be, the bound alone decides.
A program may use at most 64 MiB of HBM per device.

```python
import math
import jax
import jax.numpy as jnp
import numpy as np
from jax import lax

CX = 8
CY = 128
Z = 8
ZH = 4
KEEP = 8
SKEW = 5
SPREAD = 2
GROUPS = 32
GROUP_DEVICES = 16
NX = 256
NY = 2048
ZP = 16
BPD = 80
GCAP = 10240
N_GX = 32
N_GY = 16


GAMMA = 1.4


def draw_state(key, part):
    subkeys = jax.random.split(jax.random.fold_in(key, 11), 6)
    grid_shape = (ZP, NX, NY)
    x_frac = jnp.arange(NX, dtype=jnp.float32) / NX
    y_frac = jnp.arange(NY, dtype=jnp.float32) / NY
    heating = ((1.0 + 2.0 * x_frac)[:, None] * (1.0 + 2.0 * y_frac)[None, :])[None]
    density = jnp.exp(jax.random.uniform(subkeys[0], grid_shape, jnp.float32, -0.6, 0.6))
    velocity = jnp.clip(0.3 * jax.random.normal(subkeys[1], (3,) + grid_shape, jnp.float32), -0.9, 0.9)
    pressure = heating * jnp.exp(jax.random.uniform(subkeys[2], grid_shape, jnp.float32, -0.6, 0.6))
    momentum = density[None] * velocity
    energy = pressure / (GAMMA - 1.0) + 0.5 * density * jnp.sum(velocity * velocity, axis=0)
    return jnp.concatenate([density[None], momentum, energy[None]], axis=0).astype(jnp.float32)


def device_order(subkey):
    return jax.random.permutation(subkey, N_GY)


def block_order(subkey):
    return jax.random.permutation(subkey, 5 * (Z // 8) * (CX // 8) * (CY // 8))


def draw_counts(key, part):
    subkeys = jax.random.split(jax.random.fold_in(key, 23), 6)
    half = N_GY // 2
    blocks_dev = 5 * (Z // 8) * (CX // 8) * (CY // 8)
    pairs = blocks_dev // 2
    shifts = jax.random.randint(subkeys[0], (N_GX, half), 0, SKEW + 1)
    chosen = jax.random.randint(subkeys[1], (N_GX, 1), 0, half)
    shifts = jnp.where(jnp.arange(half)[None, :] == chosen, SKEW, shifts)
    slot_levels = jnp.concatenate([KEEP + shifts, KEEP - shifts], axis=1)
    device_perm = jax.vmap(device_order)(jax.random.split(subkeys[2], N_GX))
    levels = jnp.take_along_axis(slot_levels, jnp.argsort(device_perm, axis=1), axis=1)
    spreads = jax.random.randint(subkeys[3], (N_GX, N_GY, pairs), 0, SPREAD + 1)
    chosen_pair = jax.random.randint(subkeys[4], (N_GX, N_GY, 1), 0, pairs)
    spreads = jnp.where(jnp.arange(pairs)[None, None, :] == chosen_pair, SPREAD, spreads)
    slot_counts = jnp.concatenate([levels[..., None] + spreads, levels[..., None] - spreads], axis=2)
    block_perm = jax.vmap(block_order)(jax.random.split(subkeys[5], N_GX * N_GY)).reshape(N_GX, N_GY, blocks_dev)
    kept = jnp.take_along_axis(slot_counts, jnp.argsort(block_perm, axis=2), axis=2)
    kept = kept.reshape(N_GX, N_GY, 5, Z // 8, CX // 8, CY // 8).transpose(2, 3, 0, 4, 1, 5)
    return kept.reshape(5, Z // 8, NX // 8, NY // 8).astype(jnp.int32)


def with_ends(entries, own_key, smallest, high):
    longest = entries.shape.index(max(entries.shape))
    spots = []
    for shift in (0, 1):
        where = [jax.random.randint(jax.random.fold_in(own_key, axis), (), 0, length) for axis, length in enumerate(entries.shape)]
        where[longest] = (where[longest] + shift) % entries.shape[longest]
        spots.append(tuple(where))
    return entries.at[spots[0]].set(smallest).at[spots[1]].set(high)


def setup_inputs(seed: int = 0) -> dict:
    key_list = jax.random.split(jax.random.key(seed), 4)
    return {
        "state": draw_state(jax.random.fold_in(key_list[3], 71), 0),
        "counts": draw_counts(jax.random.fold_in(key_list[3], 71), 0),
        "aggregator": with_ends(jax.random.randint(key_list[2], (GROUPS,), 0, GROUP_DEVICES), jax.random.fold_in(key_list[2], 1), 0, GROUP_DEVICES - 1).astype(jnp.int32),
    }


GAMMA = 1.4
COURANT = 0.1

def minmod(slope_one, slope_two):
    return 0.5 * (jnp.sign(slope_one) + jnp.sign(slope_two)) * jnp.minimum(jnp.abs(slope_one), jnp.abs(slope_two))

def primitive(conserved):
    density = conserved[0]
    velocity = conserved[1:4] / density
    pressure = (GAMMA - 1.0) * (conserved[4] - 0.5 * lax.optimization_barrier(jnp.sum(conserved[1:4] * velocity, axis=0)))
    return jnp.concatenate([density[None], velocity, pressure[None]], axis=0)

def face_terms(prims, component):
    density = prims[0]
    velocity = prims[1:4]
    pressure = prims[4]
    normal_speed = velocity[component]
    energy = pressure / (GAMMA - 1.0) + 0.5 * density * lax.optimization_barrier(jnp.sum(velocity * velocity, axis=0))
    conserved = jnp.concatenate([density[None], density * velocity, energy[None]], axis=0)
    rows = [density * normal_speed]
    for index in range(3):
        term = density * velocity[index] * normal_speed
        if index == component:
            term = term + pressure
        rows.append(term)
    rows.append((energy + pressure) * normal_speed)
    fluxes = jnp.stack(rows, axis=0)
    signal = jnp.abs(normal_speed) + jnp.sqrt(GAMMA * pressure / density)
    return (conserved, fluxes, signal)

def axis_term(prims, spatial, component):
    length = prims.shape[spatial]

    def cut(start, stop):
        return lax.slice_in_dim(prims, start, stop, axis=spatial)
    centres = cut(1, length - 1)
    slopes = minmod(centres - cut(0, length - 2), cut(2, length) - centres)
    state_left = lax.slice_in_dim(centres + 0.5 * slopes, 0, length - 3, axis=spatial)
    state_right = lax.slice_in_dim(centres - 0.5 * slopes, 1, length - 2, axis=spatial)
    cons_left, flux_left, signal_left = face_terms(state_left, component)
    cons_right, flux_right, signal_right = face_terms(state_right, component)
    dissipation = jnp.maximum(signal_left, signal_right)
    fluxes = 0.5 * (flux_left + flux_right) - 0.5 * dissipation * (cons_right - cons_left)
    return lax.slice_in_dim(fluxes, 1, length - 3, axis=spatial) - lax.slice_in_dim(fluxes, 0, length - 4, axis=spatial)

def tendency(padded):
    prims = primitive(padded)
    along_z = axis_term(prims[:, :, 2:-2, 2:-2], 1, 2)
    along_x = axis_term(prims[:, 2:-2, :, 2:-2], 2, 0)
    along_y = axis_term(prims[:, 2:-2, 2:-2, :], 3, 1)
    return -(along_z + along_x + along_y)

def wave_max(conserved):
    prims = primitive(conserved)
    sound = jnp.sqrt(GAMMA * prims[4] / prims[0])
    return jnp.max(lax.optimization_barrier(jnp.max(jnp.abs(prims[1:4]), axis=0)) + sound)

def cosine_table():
    sample = jnp.arange(8, dtype=jnp.float32)
    freq = sample[:, None]
    table = jnp.cos(math.pi * (2.0 * sample[None, :] + 1.0) * freq / 16.0)
    weights = jnp.where(freq == 0, math.sqrt(0.125), 0.5)
    return table * weights

def rank_order():
    flat = np.arange(512)
    level = flat // 64 + flat // 8 % 8 + flat % 8
    keys = level * 512 + flat
    return np.argsort(keys, kind='stable').astype(np.int32)

def encode(fields):
    table = cosine_table()
    nfield, planes, xcells, ycells = fields.shape
    blocks = fields.reshape(nfield, planes // 8, 8, xcells // 8, 8, ycells // 8, 8)
    trans = jnp.einsum('kz,fazbxcy->fakbxcy', table, blocks, precision=lax.Precision.HIGHEST)
    trans = jnp.einsum('lx,fakbxcy->fakblcy', table, trans, precision=lax.Precision.HIGHEST)
    trans = jnp.einsum('my,fakblcy->fakblcm', table, trans, precision=lax.Precision.HIGHEST)
    trans = trans.transpose(0, 1, 3, 5, 2, 4, 6).reshape(nfield, planes // 8, xcells // 8, ycells // 8, 512)
    return trans[..., rank_order()]

def wrap_slab(fields, x_start, margin):
    columns = (x_start - margin + jnp.arange(CX + 2 * margin, dtype=jnp.int32)) % NX
    slab = jnp.take(fields, columns, axis=2)
    return jnp.concatenate([slab[..., NY - margin:], slab, slab[..., :margin]], axis=3)

def reference(state, counts, aggregator):
    step_ratio = COURANT / wave_max(state[:, ZH:ZH + Z])
    group_ids = jnp.arange(N_GX, dtype=jnp.int32)

    def first_slab(group):
        slab = wrap_slab(state, group * CX, 2)
        return slab[:, 2:-2, 2:-2, 2:-2] + step_ratio * tendency(slab)
    section_one = lax.map(first_slab, group_ids)
    section_one = jnp.moveaxis(section_one, 0, 2).reshape(5, ZP - 4, NX, NY)

    def second_slab(group):
        slab = wrap_slab(section_one, group * CX, 2)
        own = lax.dynamic_slice_in_dim(state[:, ZH:ZH + Z], group * CX, CX, axis=2)
        return 0.5 * own + 0.5 * (slab[:, 2:-2, 2:-2, 2:-2] + step_ratio * tendency(slab))
    advanced = lax.map(second_slab, group_ids)
    advanced = jnp.moveaxis(advanced, 0, 2).reshape(5, Z, NX, NY)
    coded = encode(advanced)
    values = coded.reshape(5, Z // 8, N_GX, CX // 8, N_GY, CY // 8, 512).transpose(2, 4, 0, 1, 3, 5, 6).reshape(N_GX, N_GY, BPD, 512)
    kept = counts.reshape(5, Z // 8, N_GX, CX // 8, N_GY, CY // 8).transpose(2, 4, 0, 1, 3, 5).reshape(N_GX, N_GY, BPD)
    totals = lax.optimization_barrier(jnp.sum(kept, axis=2))
    offsets = jnp.cumsum(kept, axis=2) - kept
    turn_rank = (jnp.arange(N_GY, dtype=jnp.int32)[None, :] - aggregator[:, None]) % N_GY
    earlier = (turn_rank[:, None, :] < turn_rank[:, :, None]).astype(jnp.int32)
    dev_offsets = lax.optimization_barrier(jnp.sum(earlier * totals[:, None, :], axis=2))
    rank_index = jnp.arange(512, dtype=jnp.int32)
    positions = dev_offsets[:, :, None, None] + offsets[:, :, :, None] + rank_index[None, None, None, :]
    is_kept = rank_index[None, None, None, :] < kept[:, :, :, None]
    group_base = (jnp.arange(N_GX, dtype=jnp.int32) * GCAP)[:, None, None, None]
    targets = jnp.where(is_kept, group_base + positions, N_GX * GCAP).astype(jnp.int32)
    stream = jnp.zeros((N_GX * GCAP,), jnp.float32).at[targets.reshape(-1)].set(values.reshape(-1), mode='drop')
    stream = stream.reshape(N_GX, GCAP)
    is_leader = jnp.arange(N_GY, dtype=jnp.int32)[None, :, None] == aggregator[:, None, None]
    snapshot = jnp.where(is_leader, stream[:, None, :], jnp.zeros((), jnp.float32))
    return (advanced, snapshot)
```

```python
import functools
import math

import jax
import jax.numpy as jnp
import numpy as np
from jax import lax
from jax.experimental import pallas as pl
from jax.experimental.pallas import tpu as pltpu
from jax.sharding import PartitionSpec as P

MESH = pl.DeviceIdType.MESH
F32 = jnp.float32
HIGHEST = lax.Precision.HIGHEST
GAMMA = 1.4
COURANT = 0.1
INNER = {32: 4, 4: 2}
PAIR = 2
CORNERS = [(0, -1), (0, 1), (1, -1), (-1, -1), (1, 1), (-1, 1)]
CHUNKS = [[((0, 0), 4), ((0, 1), 3), ((0, 3), 1)], [((0, 2), 2), ((1, 0), 3), ((1, 1), 1), ((2, 0), 1)]]
COMBOS = [c for chunk in CHUNKS for c, _ in chunk]


def cosine_np():
    k = np.arange(8)[:, None]
    n = np.arange(8)[None, :]
    w = np.where(k == 0, math.sqrt(0.125), 0.5)
    return np.cos(math.pi * (2 * n + 1) * k / 16.0) * w


def rank_of():
    flat = np.arange(512)
    keys = (flat // 64 + flat // 8 % 8 + flat % 8) * 512 + flat
    order = np.argsort(keys, kind="stable")
    rank = np.empty(512, np.int64)
    rank[order] = np.arange(512)
    return rank.reshape(8, 8, 8)


def tables():
    c = cosine_np()
    rank = rank_of()
    first = np.zeros((56, 320), np.float32)
    for i, (kz, kx) in enumerate(COMBOS):
        for f in range(5):
            first[i * 8 + f, f * 64 : f * 64 + 64] = np.outer(c[kz], c[kx]).reshape(64)
    second = np.zeros((len(COMBOS) * 128, 128), np.float32)
    ranks = np.full((2, 128), 1000, np.int32)
    row = 0
    for k, chunk in enumerate(CHUNKS):
        slot = 0
        for (kz, kx), n in chunk:
            for ky in range(n):
                for b in range(16):
                    second[row * 128 + b * 8 : row * 128 + b * 8 + 8, slot * 16 + b] = c[ky]
                ranks[k, slot * 16 : slot * 16 + 16] = rank[kz, kx, ky]
                slot += 1
            row += 1
    b = np.arange(16)[:, None]
    lane = np.arange(128)[None, :] % 16
    count = np.concatenate([(b < lane), (b == lane), np.ones((16, 128))], axis=1).astype(np.float32)
    return first, second, ranks, count


def half_slope(a, b):
    return 0.5 * (jnp.maximum(jnp.minimum(a, b), 0.0) + jnp.minimum(jnp.maximum(a, b), 0.0))


def prims_of(cons):
    rho, mx, my, mz, en = cons
    inv = 1.0 / rho
    u, v, w = mx * inv, my * inv, mz * inv
    p = (GAMMA - 1.0) * (en - 0.5 * (mx * u + my * v + mz * w))
    return [rho, u, v, w, p]


def side_terms(q, comp):
    rho, p = q[0], q[4]
    vel = q[1:4]
    vn = vel[comp]
    mom = [rho * x for x in vel]
    en = p * (1.0 / (GAMMA - 1.0)) + 0.5 * (mom[0] * vel[0] + mom[1] * vel[1] + mom[2] * vel[2])
    rows = [mom[comp]]
    for i in range(3):
        t = mom[i] * vn
        rows.append(t + p if i == comp else t)
    rows.append((en + p) * vn)
    return [rho] + mom + [en], rows, jnp.abs(vn) + jnp.sqrt(GAMMA * p / rho)


def flux2(left, right, comp):
    ul, fl, sl = side_terms(left, comp)
    ur, fr, sr = side_terms(right, comp)
    a = jnp.maximum(sl, sr)
    return [(x + y) - a * (d - c) for x, y, c, d in zip(fl, fr, ul, ur)]


def sub(a, b):
    return [x - y for x, y in zip(a, b)]


def add(a, b):
    return [x + y for x, y in zip(a, b)]


def rollto(x, shift, axis):
    n = x.shape[axis]
    shift %= n
    return pltpu.roll(x, shift, axis) if shift else x


def last(x):
    return x.ndim - 1


def iota(shape, dim):
    return lax.broadcasted_iota(jnp.int32, shape, dim)


def z_term(w):
    out_l, out_r = [], []
    for x in w:
        d = x[1:] - x[:-1]
        h = half_slope(d[1:], d[:-1])
        c = x[1:-1]
        out_l.append((c + h)[:-1])
        out_r.append((c - h)[1:])
    f = flux2(out_l, out_r, 2)
    return [x[1:] - x[:-1] for x in f]


def x_next(a, b):
    row = iota(a.shape, a.ndim - 2)
    return jnp.where(row == 7, rollto(b, -1, b.ndim - 2), rollto(a, -1, a.ndim - 2))


def x_prev(a, b):
    row = iota(a.shape, a.ndim - 2)
    return jnp.where(row == 0, rollto(b, 1, b.ndim - 2), rollto(a, 1, a.ndim - 2))


def x_terms(a, b):
    la, ra, lb, rb = [], [], [], []
    for x, y in zip(a, b):
        fx, fy = x_next(x, y) - x, x_next(y, x) - y
        hx, hy = half_slope(fx, x_prev(fx, fy)), half_slope(fy, x_prev(fy, fx))
        la.append(x + hx)
        lb.append(y + hy)
        wx, wy = x - hx, y - hy
        ra.append(x_next(wx, wy))
        rb.append(x_next(wy, wx))
    fa, fb = flux2(la, ra, 0), flux2(lb, rb, 0)
    ta = [x - x_prev(x, y) for x, y in zip(fa, fb)]
    tb = [y - x_prev(y, x) for x, y in zip(fa, fb)]
    return ta, tb


def y_term(w, e1, e2):
    lane = iota(w[0].shape, last(w[0]))
    left, right = [], []
    for x, e, g in zip(w, e1, e2):
        nxt = jnp.where(lane == 127, e, rollto(x, -1, last(x)))
        prv = jnp.where(lane == 0, e, rollto(x, 1, last(x)))
        h = half_slope(nxt - x, x - prv)
        left.append(x + h)
        right.append(jnp.where(lane == 127, g, rollto(x - h, -1, last(x))))
    f = flux2(left, right, 1)
    return [x - jnp.where(lane == 0, g, rollto(x, 1, last(x))) for x, g in zip(f, e2)]


def packed_y(w):
    left, right = [], []
    for x in w:
        d = rollto(x, -1, last(x)) - x
        h = half_slope(d, rollto(d, 1, last(d)))
        left.append(x + h)
        right.append(x - h)
    f = flux2(left, [rollto(x, -1, last(x)) for x in right], 1)
    return right, f


def packed_z(w):
    left, right = [], []
    for x in w:
        d = rollto(x, -8, last(x)) - x
        h = half_slope(d, rollto(d, 8, last(d)))
        left.append(x + h)
        right.append(x - h)
    f = flux2(left, [rollto(x, -8, last(x)) for x in right], 2)
    return [x - rollto(x, 8, last(x)) for x in f]


def edge_lanes(low, high):
    col = iota(low.shape, last(low)) % 8
    return jnp.where(col == 7, rollto(high, 3, last(high)), rollto(low, 5, last(low)))


def pack_columns(planes, zs):
    out = None
    for z in zs:
        r = rollto(planes(z), 8 * z + 4, 1)
        out = r if out is None else jnp.where(iota(r.shape, 1) // 8 == z, r, out)
    return out


def kernel(
    ngx, ngy, state, counts, agg, first, second, ranks, cmat,
    adv_out, snap_out,
    W, XH, L, Lx, Wx, E1, E2, E1x, E2x, sendx, recvx, qown, recvq, qx,
    maxsend, ry, rz, rx, tot, adv,
    ga, gb, sa, sb, gbrows, xedge, xinj,
    sem_hs, sem_hr, sem_qs, sem_qr, sem_ms, sem_mr, sem_as, sem_ar, sem_bs, sem_br,
):
    nx = INNER[ngx]
    nz = ngx // nx
    gx = lax.axis_index("gx")
    gy = lax.axis_index("gy")
    zc, xc = gx // nx, gx % nx

    def at(dx, dy):
        return ((gx + dx + ngx) % ngx, (gy + dy + ngy) % ngy)

    y_peers = [at(0, k) for k in range(1, ngy)]
    z_peers = [(((zc + k) % nz) * nx + xc, gy) for k in range(1, nz)]
    x_peers = [(zc * nx + (xc + k) % nx, gy) for k in range(1, nx)]
    halo_peers = [at(-1, 0), at(1, 0)]
    q_peers = [at(-dx, -dy) for dx, dy in CORNERS]

    barrier = pltpu.get_barrier_semaphore()
    everyone = y_peers + z_peers + x_peers + halo_peers + q_peers[2:]
    for peer in everyone:
        pl.semaphore_signal(barrier, inc=1, device_id=peer, device_id_type=MESH)

    vmax = None
    for z in range(16):
        w = prims_of([state[f, z] for f in range(5)])
        for f in range(5):
            W[f, z] = w[f]
        if 4 <= z < 12:
            c = jnp.sqrt(GAMMA * w[4] / w[0])
            s = jnp.maximum(jnp.maximum(jnp.abs(w[1]), jnp.abs(w[2])), jnp.abs(w[3])) + c
            vmax = s if vmax is None else jnp.maximum(vmax, s)
    top = jnp.max(jnp.max(vmax, axis=0, keepdims=True), axis=1, keepdims=True)

    cnt = jnp.zeros((8, 16), F32)
    row16 = iota((8, 16), 0)
    for f in range(5):
        cnt = jnp.where(row16 == f, counts[f, 0].astype(F32), cnt)
    cexp = jnp.dot(cnt, cmat[...], preferred_element_type=F32)
    total = jnp.sum(cexp[:, 256:384], axis=0, keepdims=True)
    lane1 = iota((1, 128), 1)
    maxsend[0] = jnp.where(lane1 < 64, top, total)
    ry[0] = maxsend[0]

    row8 = iota((8, 128), 0)
    for f in range(5):
        for k in range(6):
            lo, hi = state[f, 2 + k], state[f, 8 + k]
            sendx[0, f, k] = jnp.where(row8 < 4, lo, rollto(hi, 4, 0))
            sendx[1, f, k] = jnp.where(row8 < 4, rollto(lo, 4, 0), hi)
        qown[f] = pack_columns(lambda z: state[f, z], range(16))

    pl.semaphore_wait(barrier, len(everyone))

    def copies(src, bufs, peers, send, recv, base):
        return [
            pltpu.make_async_remote_copy(
                src_ref=src, dst_ref=bufs.at[k + 1], send_sem=send.at[base + k], recv_sem=recv.at[base + k],
                device_id=peer, device_id_type=MESH,
            )
            for k, peer in enumerate(peers)
        ]

    cy = copies(maxsend.at[0], ry, y_peers, sem_ms, sem_mr, 0)
    for c in cy:
        c.start()
    cq = [
        pltpu.make_async_remote_copy(
            src_ref=qown, dst_ref=recvq.at[i], send_sem=sem_qs.at[i], recv_sem=sem_qr.at[i],
            device_id=peer, device_id_type=MESH,
        )
        for i, peer in enumerate(q_peers)
    ]
    for c in cq:
        c.start()
    ch = [
        pltpu.make_async_remote_copy(
            src_ref=sendx.at[i], dst_ref=recvx.at[i], send_sem=sem_hs.at[i], recv_sem=sem_hr.at[i],
            device_id=peer, device_id_type=MESH,
        )
        for i, peer in enumerate(halo_peers)
    ]
    for c in ch:
        c.start()

    def load(ref, start, n):
        return [ref[f, pl.ds(start, n)] for f in range(5)]

    def z_main(i, carry):
        z0 = i * PAIR
        t = z_term(load(W, z0, PAIR + 4))
        for f in range(5):
            L[f, pl.ds(z0, PAIR)] = t[f]
        return carry

    lax.fori_loop(0, 12 // PAIR, z_main, 0)

    for c in cy:
        c.wait()
    best = ry[0]
    for k in range(ngy):
        if k:
            best = jnp.maximum(best, ry[k])
        tot[k : k + 1, :] = jnp.where(lane1 < 64, rollto(ry[k], 64, 1), ry[k])
    maxsend[1] = jnp.where(lane1 < 64, best, rollto(best, 64, 1))
    cz = copies(maxsend.at[1], rz, z_peers, sem_ms, sem_mr, ngy)
    for c in cz:
        c.start()

    for c in cq:
        c.wait()
    for c in ch:
        c.wait()
    for f in range(5):
        for k in range(6):
            a, b = recvx[0, f, k], recvx[1, f, k]
            XH[f, k] = jnp.where(row8 < 4, a, rollto(b, 4, 0))
            XH[f, k + 6] = jnp.where(row8 < 4, rollto(a, 4, 0), b)
    for z in range(12):
        w = prims_of([XH[f, z] for f in range(5)])
        for f in range(5):
            Wx[f, z] = w[f]
    colm = iota((8, 128), 1) % 8
    packed = []
    for f in range(5):
        q = qown[f]
        qh = pack_columns(lambda z: XH[f, z - 2], range(2, 14))
        lo = jnp.where(row8 < 4, recvq[2, f], recvq[3, f])
        hi = jnp.where(row8 < 4, recvq[4, f], recvq[5, f])
        packed.append(
            jnp.stack(
                [
                    jnp.where(colm < 4, recvq[0, f], q),
                    jnp.where(colm < 4, q, recvq[1, f]),
                    jnp.where(colm < 4, lo, qh),
                    jnp.where(colm < 4, qh, hi),
                ]
            )
        )
    pw = prims_of(packed)
    pr, pf = packed_y(pw)
    ta, _ = x_terms([x[:2] for x in pw], [x[2:] for x in pw])
    tz = packed_z([x[:2] for x in pw])
    for f in range(5):
        ty = pf[f] - rollto(pf[f], 1, 2)
        qx[0, f] = packed[f][:2]
        qx[1, f] = ta[f] + tz[f] + ty[:2]

    def inject(e1, e2, pw, pr, pf, low, high, planes, offset):
        for f in range(5):
            c1 = edge_lanes(pw[f][low], pw[f][high])
            c2 = edge_lanes(pf[f][low], pr[f][high])
            for z in planes:
                e1[f, z - offset] = rollto(c1, -(8 * z + 8), 1)
                e2[f, z - offset] = rollto(c2, -(8 * z + 8), 1)

    inject(E1, E2, pw, pr, pf, 0, 1, range(2, 14), 2)
    inject(E1x, E2x, pw, pr, pf, 2, 3, range(4, 12), 4)

    def xy_main(i, carry):
        z0 = i * PAIR
        a = load(W, z0 + 2, PAIR)
        ta, tb = x_terms(a, load(Wx, z0, PAIR))
        ty = y_term(a, load(E1, z0, PAIR), load(E2, z0, PAIR))
        for f in range(5):
            L[f, pl.ds(z0, PAIR)] = L[f, pl.ds(z0, PAIR)] + ta[f] + ty[f]
            Lx[f, pl.ds(z0, PAIR)] = tb[f]
        return carry

    lax.fori_loop(0, 12 // PAIR, xy_main, 0)

    for c in cz:
        c.wait()
    best = maxsend[1]
    for k in range(1, nz):
        best = jnp.maximum(best, rz[k])
    maxsend[2] = best
    cx = copies(maxsend.at[2], rx, x_peers, sem_ms, sem_mr, ngy + nz)
    for c in cx:
        c.start()

    def strip(i, carry):
        z0 = i * PAIR
        w = load(Wx, z0, PAIR + 4)
        tz = z_term(w)
        ty = y_term([x[2:-2] for x in w], load(E1x, z0, PAIR), load(E2x, z0, PAIR))
        for f in range(5):
            Lx[f, pl.ds(z0 + 2, PAIR)] = Lx[f, pl.ds(z0 + 2, PAIR)] + tz[f] + ty[f]
        return carry

    lax.fori_loop(0, 8 // PAIR, strip, 0)
    for f in range(5):
        for j, r in enumerate((6, 7, 0, 1)):
            for z in range(8):
                xedge[0, f, j, z : z + 1, :] = XH[f, z + 2, r : r + 1, :]
                xedge[1, f, j, z : z + 1, :] = Lx[f, z + 2, r : r + 1, :]
        for j, r in enumerate((0, 1, 7)):
            for z in range(8):
                xedge[0, f, j + 4, z : z + 1, :] = state[f, z + 4, r : r + 1, :]
                xedge[1, f, j + 4, z : z + 1, :] = L[f, z + 2, r : r + 1, :]

    me_rank = jnp.full((1, 1), (gy - agg[0] + ngy) % ngy, jnp.int32)
    nlane = ngy * 8
    slot_col = iota((ngy, nlane), 0)
    slot_row = iota((ngy, nlane), 1) // 8

    def turn(slot):
        return (gy - slot - agg[0] + 2 * ngy) & (ngy - 1)

    totals = tot[...]
    before = jnp.where(turn(slot_col) < turn(slot_row), totals[:, :nlane], 0.0)
    starts = jnp.sum(before, axis=0, keepdims=True).astype(jnp.int32)
    mine = jnp.sum(
        jnp.where(turn(iota((ngy, 128), 0)) < me_rank, totals, 0.0), axis=0, keepdims=True
    ).astype(jnp.int32)
    field_total = cexp[:, 256:384]
    upto = cexp[:, :128]
    for f in range(4):
        upto = upto + jnp.where(row8 > f, field_total[f : f + 1, :], 0.0)
    own_count = cexp[:, 128:256].astype(jnp.int32)
    base = upto.astype(jnp.int32) + (mine & 127)
    dest, spots = [], []
    for k in range(2):
        rank = ranks[k : k + 1, :]
        pos = base + rank
        keep = rank < own_count
        row_to = jnp.where(keep, pos >> 7, -1)
        lane_to = pos & 127
        for f in range(5):
            dest.append(row_to[f : f + 1, :])
            spots.append((iota((128, 128), 0) == lane_to[f : f + 1, :]).astype(F32))
    spots = jnp.concatenate(spots, axis=1)
    dest = [(iota((16, 128), 0) == d).astype(F32) for d in dest]

    for c in cx:
        c.wait()
    best = maxsend[2]
    for k in range(1, nx):
        best = jnp.maximum(best, rx[k])
    ratio = COURANT / best
    half = -0.5 * ratio

    p1 = prims_of([qx[0, f] + half * qx[1, f] for f in range(5)])
    pr, pf = packed_y(p1)
    inject(E1, E2, p1, pr, pf, 0, 1, range(4, 12), 4)
    we = prims_of([xedge[0, f] + half * xedge[1, f] for f in range(5)])
    fl, fr = [], []
    for f in range(5):
        m2, m1, p8, p9, c0, c1, c7 = [we[f][j] for j in range(7)]
        h = half_slope(c0 - m1, m1 - m2)
        g = half_slope(c1 - c0, c0 - m1)
        fl.append(m1 + h)
        fr.append(c0 - g)
        xinj[0, f] = m1
        xinj[1, f] = p8
        xinj[2, f] = p8 - half_slope(p9 - p8, p8 - c7)
    fx = flux2(fl, fr, 0)
    for f in range(5):
        xinj[3, f] = fx[f]

    def section(i, carry):
        z0 = i * PAIR
        s = [state[f, pl.ds(z0 + 2, PAIR)] + half * L[f, pl.ds(z0, PAIR)] for f in range(5)]
        w = prims_of(s)
        for f in range(5):
            L[f, pl.ds(z0, PAIR)] = s[f]
            W[f, pl.ds(z0, PAIR)] = w[f]
        return carry

    lax.fori_loop(0, 12 // PAIR, section, 0)

    def second_step(i, carry):
        z0 = i * PAIR
        w = load(W, z0, PAIR + 4)
        tz = z_term(w)
        c = [x[2:-2] for x in w]
        ty = y_term(c, load(E1, z0, PAIR), load(E2, z0, PAIR))

        def rows(j, f):
            return jnp.stack([xinj[j, f, pl.ds(z0 + d, 1), :] for d in range(PAIR)])

        row = iota(c[0].shape, 1)
        left, right, inj = [], [], []
        for f in range(5):
            x = c[f]
            nxt = jnp.where(row == 7, rows(1, f), rollto(x, -1, 1))
            prv = jnp.where(row == 0, rows(0, f), rollto(x, 1, 1))
            h = half_slope(nxt - x, x - prv)
            left.append(x + h)
            right.append(jnp.where(row == 7, rows(2, f), rollto(x - h, -1, 1)))
        fx = flux2(left, right, 0)
        for f in range(5):
            tx = fx[f] - jnp.where(row == 0, rows(3, f), rollto(fx[f], 1, 1))
            s = L[f, pl.ds(z0 + 2, PAIR)] + half * (tx + ty[f] + tz[f])
            adv[f, pl.ds(z0, PAIR)] = 0.5 * state[f, pl.ds(z0 + 4, PAIR)] + 0.5 * s
        return carry

    lax.fori_loop(0, 8 // PAIR, second_step, 0)
    adv_out[...] = adv[...]

    flat = adv[...].reshape(320, 128)
    y1 = jnp.dot(first[...], flat, precision=HIGHEST, preferred_element_type=F32)
    image = None
    col = 0
    lhs = []
    for k, chunk in enumerate(CHUNKS):
        n = len(chunk)
        y2 = jnp.concatenate([y1[(col + i) * 8 : (col + i) * 8 + 8] for i in range(n)], axis=1)
        v = jnp.dot(y2, second[col * 128 : (col + n) * 128, :], precision=HIGHEST, preferred_element_type=F32)
        col += n
        for f in range(5):
            lhs.append(dest[k * 5 + f] * v[f : f + 1, :])
    image = lax.dot_general(
        jnp.concatenate(lhs, axis=1), spots, (((1,), (1,)), ((), ())),
        precision=HIGHEST, preferred_element_type=F32,
    )
    sa[...] = image[:8]
    sb[...] = image[8:10]
    ga[0] = image[:8]
    gb[0] = image[8:10]
    ca = copies(sa, ga, y_peers, sem_as, sem_ar, 0)
    cb = copies(sb, gb, y_peers, sem_bs, sem_br, 0)
    for a, b in zip(ca, cb):
        a.start()
        b.start()

    nrow = ngy * 5
    q = iota((nrow, nlane), 0)
    lead = jnp.full((1, 1), agg[0], jnp.int32) == gy
    in_row = q - (starts >> 7)
    sel_a = jnp.where((in_row == iota((nrow, nlane), 1) % 8) & lead, 1.0, 0.0)
    q2 = iota((nrow, ngy * 2), 0)
    slot2 = iota((ngy, ngy * 2), 1) // 2
    before2 = jnp.where(turn(iota((ngy, ngy * 2), 0)) < turn(slot2), totals[:, : ngy * 2], 0.0)
    starts2 = jnp.sum(before2, axis=0, keepdims=True).astype(jnp.int32)
    sel_b = jnp.where((q2 - (starts2 >> 7) == 8 + iota((nrow, ngy * 2), 1) % 2) & lead, 1.0, 0.0)
    for a, b in zip(ca, cb):
        a.wait()
        b.wait()
    for k in range(ngy):
        gbrows[2 * k : 2 * k + 2, :] = gb[k]
    snap_out[...] = jnp.dot(
        sel_a, ga[...].reshape(ngy * 8, 128), precision=HIGHEST, preferred_element_type=F32
    ) + jnp.dot(sel_b, gbrows[...], precision=HIGHEST, preferred_element_type=F32)


def shards(ngx, ngy, state, counts, aggregator):
    nx = INNER[ngx]
    nz = ngx // nx
    first, second, ranks, cmat = tables()
    vm = pltpu.VMEM
    dma = pltpu.SemaphoreType.DMA
    nmax = ngy + nz + nx
    vmem = pl.BlockSpec(memory_space=pltpu.VMEM)
    adv, snap = pl.pallas_call(
        functools.partial(kernel, ngx, ngy),
        out_shape=(
            jax.ShapeDtypeStruct((5, 8, 8, 128), F32),
            jax.ShapeDtypeStruct((ngy * 5, 128), F32),
        ),
        in_specs=[vmem, vmem, pl.BlockSpec(memory_space=pltpu.SMEM)] + [vmem] * 4,
        out_specs=(vmem, vmem),
        scratch_shapes=[
            vm((5, 16, 8, 128), F32),
            vm((5, 12, 8, 128), F32),
            vm((5, 12, 8, 128), F32),
            vm((5, 12, 8, 128), F32),
            vm((5, 12, 8, 128), F32),
            vm((5, 12, 8, 128), F32),
            vm((5, 12, 8, 128), F32),
            vm((5, 8, 8, 128), F32),
            vm((5, 8, 8, 128), F32),
            vm((2, 5, 6, 8, 128), F32),
            vm((2, 5, 6, 8, 128), F32),
            vm((5, 8, 128), F32),
            vm((6, 5, 8, 128), F32),
            vm((2, 5, 2, 8, 128), F32),
            vm((3, 1, 128), F32),
            vm((ngy, 1, 128), F32),
            vm((nz, 1, 128), F32),
            vm((nx, 1, 128), F32),
            vm((ngy, 128), F32),
            vm((5, 8, 8, 128), F32),
            vm((ngy, 8, 128), F32),
            vm((ngy, 2, 128), F32),
            vm((8, 128), F32),
            vm((2, 128), F32),
            vm((ngy * 2, 128), F32),
            vm((2, 5, 7, 8, 128), F32),
            vm((4, 5, 8, 128), F32),
            dma((2,)), dma((2,)), dma((6,)), dma((6,)), dma((nmax,)), dma((nmax,)),
            dma((ngy,)), dma((ngy,)), dma((ngy,)), dma((ngy,)),
        ],
        compiler_params=pltpu.CompilerParams(collective_id=0, has_side_effects=True),
        name="step",
    )(state, counts, aggregator, first, second, ranks, cmat)
    return adv, snap.reshape(1, 1, ngy * 640)


def solution(mesh):
    ngx, ngy = mesh.shape["gx"], mesh.shape["gy"]
    placed = (P(None, None, "gx", "gy"), P(None, None, "gx", "gy"), P("gx"))
    return jax.shard_map(
        functools.partial(shards, ngx, ngy),
        mesh=mesh,
        in_specs=placed,
        out_specs=(P(None, None, "gx", "gy"), P("gx", "gy", None)),
        check_vma=False,
    )
```

```python
import functools
import math

import jax
import jax.numpy as jnp
import numpy as np
from jax import lax
from jax.experimental import pallas as pl
from jax.experimental.pallas import tpu as pltpu
from jax.sharding import PartitionSpec as P

MESH = pl.DeviceIdType.MESH
F32 = jnp.float32
BF16 = jnp.bfloat16
GAMMA = 1.4
COURANT = 0.1
INNER = {32: 4, 4: 2}
PAIR = 2
CORNERS = [(0, -1), (0, 1), (1, -1), (-1, -1), (1, 1), (-1, 1)]
CHUNKS = [[((0, 0), 4), ((0, 1), 3), ((0, 3), 1)], [((0, 2), 2), ((1, 0), 3), ((1, 1), 1), ((2, 0), 1)]]
COMBOS = [c for chunk in CHUNKS for c, _ in chunk]


def cosine_np():
    k = np.arange(8)[:, None]
    n = np.arange(8)[None, :]
    w = np.where(k == 0, math.sqrt(0.125), 0.5)
    return np.cos(math.pi * (2 * n + 1) * k / 16.0) * w


def rank_of():
    flat = np.arange(512)
    keys = (flat // 64 + flat // 8 % 8 + flat % 8) * 512 + flat
    order = np.argsort(keys, kind="stable")
    rank = np.empty(512, np.int64)
    rank[order] = np.arange(512)
    return rank.reshape(8, 8, 8)


def tables():
    c = cosine_np()
    rank = rank_of()
    first = np.zeros((56, 320), np.float32)
    for i, (kz, kx) in enumerate(COMBOS):
        for f in range(5):
            first[i * 8 + f, f * 64 : f * 64 + 64] = np.outer(c[kz], c[kx]).reshape(64)
    second = np.zeros((len(COMBOS) * 128, 128), np.float32)
    ranks = np.full((2, 128), 1000, np.int32)
    row = 0
    for k, chunk in enumerate(CHUNKS):
        slot = 0
        for (kz, kx), n in chunk:
            for ky in range(n):
                for b in range(16):
                    second[row * 128 + b * 8 : row * 128 + b * 8 + 8, slot * 16 + b] = c[ky]
                ranks[k, slot * 16 : slot * 16 + 16] = rank[kz, kx, ky]
                slot += 1
            row += 1
    b = np.arange(16)[:, None]
    lane = np.arange(128)[None, :] % 16
    count = np.concatenate([(b < lane), (b == lane), np.ones((16, 128))], axis=1).astype(np.float32)
    first_hi = first.astype(BF16)
    first_lo = (first - first_hi.astype(np.float32)).astype(BF16)
    second_hi = second.astype(BF16)
    second_lo = (second - second_hi.astype(np.float32)).astype(BF16)
    return np.concatenate([first_hi, first_lo]), np.stack([second_hi, second_lo]), ranks, count


def half_slope(a, b):
    return 0.5 * (jnp.maximum(jnp.minimum(a, b), 0.0) + jnp.minimum(jnp.maximum(a, b), 0.0))


def prims_of(cons):
    rho, mx, my, mz, en = cons
    inv = 1.0 / rho
    u, v, w = mx * inv, my * inv, mz * inv
    p = (GAMMA - 1.0) * (en - 0.5 * (mx * u + my * v + mz * w))
    return [rho, u, v, w, p]


def side_terms(q, comp):
    rho, p = q[0], q[4]
    vel = q[1:4]
    vn = vel[comp]
    mom = [rho * x for x in vel]
    en = p * (1.0 / (GAMMA - 1.0)) + 0.5 * (mom[0] * vel[0] + mom[1] * vel[1] + mom[2] * vel[2])
    rows = [mom[comp]]
    for i in range(3):
        t = mom[i] * vn
        rows.append(t + p if i == comp else t)
    rows.append((en + p) * vn)
    return [rho] + mom + [en], rows, jnp.abs(vn) + jnp.sqrt(GAMMA * p / rho)


def flux2(left, right, comp):
    ul, fl, sl = side_terms(left, comp)
    ur, fr, sr = side_terms(right, comp)
    a = jnp.maximum(sl, sr)
    return [(x + y) - a * (d - c) for x, y, c, d in zip(fl, fr, ul, ur)]


def sub(a, b):
    return [x - y for x, y in zip(a, b)]


def add(a, b):
    return [x + y for x, y in zip(a, b)]


def split(x):
    hi = x.astype(BF16)
    return hi, (x - hi.astype(F32)).astype(BF16)


def mm(a, b):
    return jnp.dot(a, b, preferred_element_type=F32)


def rollto(x, shift, axis):
    n = x.shape[axis]
    shift %= n
    return pltpu.roll(x, shift, axis) if shift else x


def last(x):
    return x.ndim - 1


def iota(shape, dim):
    return lax.broadcasted_iota(jnp.int32, shape, dim)


def z_term(w):
    out_l, out_r = [], []
    for x in w:
        d = x[1:] - x[:-1]
        h = half_slope(d[1:], d[:-1])
        c = x[1:-1]
        out_l.append((c + h)[:-1])
        out_r.append((c - h)[1:])
    f = flux2(out_l, out_r, 2)
    return [x[1:] - x[:-1] for x in f]


def x_next(a, b):
    row = iota(a.shape, a.ndim - 2)
    return jnp.where(row == 7, rollto(b, -1, b.ndim - 2), rollto(a, -1, a.ndim - 2))


def x_prev(a, b):
    row = iota(a.shape, a.ndim - 2)
    return jnp.where(row == 0, rollto(b, 1, b.ndim - 2), rollto(a, 1, a.ndim - 2))


def x_terms(a, b):
    la, ra, lb, rb = [], [], [], []
    for x, y in zip(a, b):
        fx, fy = x_next(x, y) - x, x_next(y, x) - y
        hx, hy = half_slope(fx, x_prev(fx, fy)), half_slope(fy, x_prev(fy, fx))
        la.append(x + hx)
        lb.append(y + hy)
        wx, wy = x - hx, y - hy
        ra.append(x_next(wx, wy))
        rb.append(x_next(wy, wx))
    fa, fb = flux2(la, ra, 0), flux2(lb, rb, 0)
    ta = [x - x_prev(x, y) for x, y in zip(fa, fb)]
    tb = [y - x_prev(y, x) for x, y in zip(fa, fb)]
    return ta, tb


def y_term(w, e1, e2):
    lane = iota(w[0].shape, last(w[0]))
    left, right = [], []
    for x, e, g in zip(w, e1, e2):
        nxt = jnp.where(lane == 127, e, rollto(x, -1, last(x)))
        prv = jnp.where(lane == 0, e, rollto(x, 1, last(x)))
        h = half_slope(nxt - x, x - prv)
        left.append(x + h)
        right.append(jnp.where(lane == 127, g, rollto(x - h, -1, last(x))))
    f = flux2(left, right, 1)
    return [x - jnp.where(lane == 0, g, rollto(x, 1, last(x))) for x, g in zip(f, e2)]


def packed_y(w):
    left, right = [], []
    for x in w:
        d = rollto(x, -1, last(x)) - x
        h = half_slope(d, rollto(d, 1, last(d)))
        left.append(x + h)
        right.append(x - h)
    f = flux2(left, [rollto(x, -1, last(x)) for x in right], 1)
    return right, f


def packed_z(w):
    left, right = [], []
    for x in w:
        d = rollto(x, -8, last(x)) - x
        h = half_slope(d, rollto(d, 8, last(d)))
        left.append(x + h)
        right.append(x - h)
    f = flux2(left, [rollto(x, -8, last(x)) for x in right], 2)
    return [x - rollto(x, 8, last(x)) for x in f]


def edge_lanes(low, high):
    col = iota(low.shape, last(low)) % 8
    return jnp.where(col == 7, rollto(high, 3, last(high)), rollto(low, 5, last(low)))


def pack_columns(planes, zs):
    out = None
    for z in zs:
        r = rollto(planes(z), 8 * z + 4, 1)
        out = r if out is None else jnp.where(iota(r.shape, 1) // 8 == z, r, out)
    return out


def kernel(
    ngx, ngy, state_in, counts_in, agg_in, first_in, second_in, ranks_in, cmat_in,
    adv, snap_out,
    state, counts, agg, first, second, ranks, cmat, sem_in,
    W, XH, L, Lx, Wx, E1, E2, E1x, E2x, sendx, recvx, qown, recvq, qx,
    maxsend, ry, rz, rx, tot,
    ga, gb, sa, sb, gbrows, xedge, xinj,
    sem_hs, sem_hr, sem_qs, sem_qr, sem_ms, sem_mr, sem_as, sem_ar, sem_bs, sem_br,
):
    loads = [
        pltpu.make_async_copy(src, dst, sem_in.at[i])
        for i, (src, dst) in enumerate(
            [(state_in.at[:, 4:12], state.at[:, 4:12]), (counts_in, counts), (cmat_in, cmat)]
            + [(state_in.at[:, 0:4], state.at[:, 0:4]), (state_in.at[:, 12:16], state.at[:, 12:16])]
            + [(agg_in, agg), (ranks_in, ranks), (first_in, first), (second_in, second)]
        )
    ]
    for c in loads:
        c.start()

    nx = INNER[ngx]
    nz = ngx // nx
    gx = lax.axis_index("gx")
    gy = lax.axis_index("gy")
    zc, xc = lax.div(gx, nx), lax.rem(gx, nx)

    def at(dx, dy):
        x = lax.rem(gx + (dx % ngx), ngx) if dx else gx
        y = lax.rem(gy + (dy % ngy), ngy) if dy else gy
        return (x, y)

    y_peers = [at(0, k) for k in range(1, ngy)]
    z_peers = [(lax.rem(zc + k, nz) * nx + xc, gy) for k in range(1, nz)]
    x_peers = [(zc * nx + lax.rem(xc + k, nx), gy) for k in range(1, nx)]
    halo_peers = [at(-1, 0), at(1, 0)]
    q_peers = [at(-dx, -dy) for dx, dy in CORNERS]

    barrier = pltpu.get_barrier_semaphore()
    everyone = y_peers + z_peers + x_peers + halo_peers + q_peers[2:]
    for peer in everyone:
        pl.semaphore_signal(barrier, inc=1, device_id=peer, device_id_type=MESH)

    for c in loads[:3]:
        c.wait()
    vmax = None
    for z in range(4, 12):
        w = prims_of([state[f, z] for f in range(5)])
        for f in range(5):
            W[f, z] = w[f]
        c = jnp.sqrt(GAMMA * w[4] / w[0])
        s = jnp.maximum(jnp.maximum(jnp.abs(w[1]), jnp.abs(w[2])), jnp.abs(w[3])) + c
        vmax = s if vmax is None else jnp.maximum(vmax, s)
    top = jnp.max(jnp.max(vmax, axis=0, keepdims=True), axis=1, keepdims=True)

    cnt = jnp.zeros((8, 16), F32)
    row16 = iota((8, 16), 0)
    for f in range(5):
        cnt = jnp.where(row16 == f, counts[f, 0].astype(F32), cnt)
    cexp = jnp.dot(cnt, cmat[...], preferred_element_type=F32)
    total = jnp.sum(cexp[:, 256:384], axis=0, keepdims=True)
    lane1 = iota((1, 128), 1)
    maxsend[0] = jnp.where(lane1 < 64, top, total)
    ry[0] = maxsend[0]

    pl.semaphore_wait(barrier, len(everyone))

    def copies(src, bufs, peers, send, recv, base):
        return [
            pltpu.make_async_remote_copy(
                src_ref=src, dst_ref=bufs.at[k + 1], send_sem=send.at[base + k], recv_sem=recv.at[base + k],
                device_id=peer, device_id_type=MESH,
            )
            for k, peer in enumerate(peers)
        ]

    cy = copies(maxsend.at[0], ry, y_peers, sem_ms, sem_mr, 0)
    for c in cy:
        c.start()
    for c in loads[3:]:
        c.wait()
    row8 = iota((8, 128), 0)
    for f in range(5):
        for k in range(6):
            lo, hi = state[f, 2 + k], state[f, 8 + k]
            sendx[0, f, k] = jnp.where(row8 < 4, lo, rollto(hi, 4, 0))
            sendx[1, f, k] = jnp.where(row8 < 4, rollto(lo, 4, 0), hi)
        qown[f] = pack_columns(lambda z: state[f, z], range(16))
    cq = [
        pltpu.make_async_remote_copy(
            src_ref=qown, dst_ref=recvq.at[i], send_sem=sem_qs.at[i], recv_sem=sem_qr.at[i],
            device_id=peer, device_id_type=MESH,
        )
        for i, peer in enumerate(q_peers)
    ]
    for c in cq:
        c.start()
    ch = [
        pltpu.make_async_remote_copy(
            src_ref=sendx.at[i], dst_ref=recvx.at[i], send_sem=sem_hs.at[i], recv_sem=sem_hr.at[i],
            device_id=peer, device_id_type=MESH,
        )
        for i, peer in enumerate(halo_peers)
    ]
    for c in ch:
        c.start()

    for z in (*range(0, 4), *range(12, 16)):
        w = prims_of([state[f, z] for f in range(5)])
        for f in range(5):
            W[f, z] = w[f]

    def load(ref, start, n):
        return [ref[f, pl.ds(start, n)] for f in range(5)]

    def z_main(i, carry):
        z0 = i * PAIR
        t = z_term(load(W, z0, PAIR + 4))
        for f in range(5):
            L[f, pl.ds(z0, PAIR)] = t[f]
        return carry

    lax.fori_loop(0, 12 // PAIR, z_main, 0)

    for c in cy:
        c.wait()
    best = ry[0]
    for k in range(ngy):
        if k:
            best = jnp.maximum(best, ry[k])
        tot[k : k + 1, :] = jnp.where(lane1 < 64, rollto(ry[k], 64, 1), ry[k])
    maxsend[1] = jnp.where(lane1 < 64, best, rollto(best, 64, 1))
    cz = copies(maxsend.at[1], rz, z_peers, sem_ms, sem_mr, ngy)
    for c in cz:
        c.start()

    for c in cq:
        c.wait()
    for c in ch:
        c.wait()
    for f in range(5):
        for k in range(6):
            a, b = recvx[0, f, k], recvx[1, f, k]
            XH[f, k] = jnp.where(row8 < 4, a, rollto(b, 4, 0))
            XH[f, k + 6] = jnp.where(row8 < 4, rollto(a, 4, 0), b)
    for z in range(12):
        w = prims_of([XH[f, z] for f in range(5)])
        for f in range(5):
            Wx[f, z] = w[f]
    colm = iota((8, 128), 1) % 8
    packed = []
    for f in range(5):
        q = qown[f]
        qh = pack_columns(lambda z: XH[f, z - 2], range(2, 14))
        lo = jnp.where(row8 < 4, recvq[2, f], recvq[3, f])
        hi = jnp.where(row8 < 4, recvq[4, f], recvq[5, f])
        packed.append(
            jnp.stack(
                [
                    jnp.where(colm < 4, recvq[0, f], q),
                    jnp.where(colm < 4, q, recvq[1, f]),
                    jnp.where(colm < 4, lo, qh),
                    jnp.where(colm < 4, qh, hi),
                ]
            )
        )
    pw = prims_of(packed)
    pr, pf = packed_y(pw)
    ta, _ = x_terms([x[:2] for x in pw], [x[2:] for x in pw])
    tz = packed_z([x[:2] for x in pw])
    for f in range(5):
        ty = pf[f] - rollto(pf[f], 1, 2)
        qx[0, f] = packed[f][:2]
        qx[1, f] = ta[f] + tz[f] + ty[:2]

    def inject(e1, e2, pw, pr, pf, low, high, planes, offset):
        for f in range(5):
            c1 = edge_lanes(pw[f][low], pw[f][high])
            c2 = edge_lanes(pf[f][low], pr[f][high])
            for z in planes:
                e1[f, z - offset] = rollto(c1, -(8 * z + 8), 1)
                e2[f, z - offset] = rollto(c2, -(8 * z + 8), 1)

    inject(E1, E2, pw, pr, pf, 0, 1, range(2, 14), 2)
    inject(E1x, E2x, pw, pr, pf, 2, 3, range(4, 12), 4)

    def xy_main(i, carry):
        z0 = i * PAIR
        a = load(W, z0 + 2, PAIR)
        ta, tb = x_terms(a, load(Wx, z0, PAIR))
        ty = y_term(a, load(E1, z0, PAIR), load(E2, z0, PAIR))
        for f in range(5):
            L[f, pl.ds(z0, PAIR)] = L[f, pl.ds(z0, PAIR)] + ta[f] + ty[f]
            Lx[f, pl.ds(z0, PAIR)] = tb[f]
        return carry

    lax.fori_loop(0, 12 // PAIR, xy_main, 0)

    for c in cz:
        c.wait()
    best = maxsend[1]
    for k in range(1, nz):
        best = jnp.maximum(best, rz[k])
    maxsend[2] = best
    cx = copies(maxsend.at[2], rx, x_peers, sem_ms, sem_mr, ngy + nz)
    for c in cx:
        c.start()

    def strip(i, carry):
        z0 = i * PAIR
        w = load(Wx, z0, PAIR + 4)
        tz = z_term(w)
        ty = y_term([x[2:-2] for x in w], load(E1x, z0, PAIR), load(E2x, z0, PAIR))
        for f in range(5):
            Lx[f, pl.ds(z0 + 2, PAIR)] = Lx[f, pl.ds(z0 + 2, PAIR)] + tz[f] + ty[f]
        return carry

    lax.fori_loop(0, 8 // PAIR, strip, 0)
    for f in range(5):
        for j, r in enumerate((6, 7, 0, 1)):
            for z in range(8):
                xedge[0, f, j, z : z + 1, :] = XH[f, z + 2, r : r + 1, :]
                xedge[1, f, j, z : z + 1, :] = Lx[f, z + 2, r : r + 1, :]
        for j, r in enumerate((0, 1, 7)):
            for z in range(8):
                xedge[0, f, j + 4, z : z + 1, :] = state[f, z + 4, r : r + 1, :]
                xedge[1, f, j + 4, z : z + 1, :] = L[f, z + 2, r : r + 1, :]

    me_rank = jnp.full((1, 1), (gy - agg[0] + ngy) % ngy, jnp.int32)
    nlane = ngy * 8
    slot_col = iota((ngy, nlane), 0)
    slot_row = iota((ngy, nlane), 1) // 8

    def turn(slot):
        return (gy - slot - agg[0] + 2 * ngy) & (ngy - 1)

    totals = tot[...]
    before = jnp.where(turn(slot_col) < turn(slot_row), totals[:, :nlane], 0.0)
    starts = jnp.sum(before, axis=0, keepdims=True).astype(jnp.int32)
    mine = jnp.sum(
        jnp.where(turn(iota((ngy, 128), 0)) < me_rank, totals, 0.0), axis=0, keepdims=True
    ).astype(jnp.int32)
    field_total = cexp[:, 256:384]
    upto = cexp[:, :128]
    for f in range(4):
        upto = upto + jnp.where(row8 > f, field_total[f : f + 1, :], 0.0)
    own_count = cexp[:, 128:256].astype(jnp.int32)
    base = upto.astype(jnp.int32) + (mine & 127)
    dest, spots = [], []
    for k in range(2):
        rank = ranks[k : k + 1, :]
        pos = base + rank
        keep = rank < own_count
        row_to = jnp.where(keep, pos >> 7, -1)
        lane_to = pos & 127
        for f in range(5):
            dest.append(row_to[f : f + 1, :])
            spots.append((iota((128, 128), 0) == lane_to[f : f + 1, :]).astype(F32).astype(BF16))
    spots = jnp.concatenate(spots, axis=1)
    dest = [(iota((16, 128), 0) == d).astype(F32) for d in dest]

    for c in cx:
        c.wait()
    best = maxsend[2]
    for k in range(1, nx):
        best = jnp.maximum(best, rx[k])
    ratio = COURANT / best
    half = -0.5 * ratio

    p1 = prims_of([qx[0, f] + half * qx[1, f] for f in range(5)])
    pr, pf = packed_y(p1)
    inject(E1, E2, p1, pr, pf, 0, 1, range(4, 12), 4)
    we = prims_of([xedge[0, f] + half * xedge[1, f] for f in range(5)])
    fl, fr = [], []
    for f in range(5):
        m2, m1, p8, p9, c0, c1, c7 = [we[f][j] for j in range(7)]
        h = half_slope(c0 - m1, m1 - m2)
        g = half_slope(c1 - c0, c0 - m1)
        fl.append(m1 + h)
        fr.append(c0 - g)
        xinj[0, f] = m1
        xinj[1, f] = p8
        xinj[2, f] = p8 - half_slope(p9 - p8, p8 - c7)
    fx = flux2(fl, fr, 0)
    for f in range(5):
        xinj[3, f] = fx[f]

    def section(i, carry):
        z0 = i * PAIR
        s = [state[f, pl.ds(z0 + 2, PAIR)] + half * L[f, pl.ds(z0, PAIR)] for f in range(5)]
        w = prims_of(s)
        for f in range(5):
            L[f, pl.ds(z0, PAIR)] = s[f]
            W[f, pl.ds(z0, PAIR)] = w[f]
        return carry

    lax.fori_loop(0, 12 // PAIR, section, 0)

    def second_step(i, carry):
        z0 = i * PAIR
        w = load(W, z0, PAIR + 4)
        tz = z_term(w)
        c = [x[2:-2] for x in w]
        ty = y_term(c, load(E1, z0, PAIR), load(E2, z0, PAIR))

        def rows(j, f):
            return jnp.stack([xinj[j, f, pl.ds(z0 + d, 1), :] for d in range(PAIR)])

        row = iota(c[0].shape, 1)
        left, right, inj = [], [], []
        for f in range(5):
            x = c[f]
            nxt = jnp.where(row == 7, rows(1, f), rollto(x, -1, 1))
            prv = jnp.where(row == 0, rows(0, f), rollto(x, 1, 1))
            h = half_slope(nxt - x, x - prv)
            left.append(x + h)
            right.append(jnp.where(row == 7, rows(2, f), rollto(x - h, -1, 1)))
        fx = flux2(left, right, 0)
        for f in range(5):
            tx = fx[f] - jnp.where(row == 0, rows(3, f), rollto(fx[f], 1, 1))
            s = L[f, pl.ds(z0 + 2, PAIR)] + half * (tx + ty[f] + tz[f])
            adv[f, pl.ds(z0, PAIR)] = 0.5 * state[f, pl.ds(z0 + 4, PAIR)] + 0.5 * s
        return carry

    lax.fori_loop(0, 8 // PAIR, second_step, 0)

    hi, lo = split(adv[...].reshape(320, 128))
    y1 = mm(first[...], hi)
    y1 = y1[:56] + y1[56:] + mm(first[:56, :], lo)
    col = 0
    lhs_hi, lhs_lo = [], []
    for k, chunk in enumerate(CHUNKS):
        n = len(chunk)
        y2 = jnp.concatenate([y1[(col + i) * 8 : (col + i) * 8 + 8] for i in range(n)], axis=1)
        hi, lo = split(y2)
        rows = slice(col * 128, (col + n) * 128)
        v = mm(hi, second[0, rows, :]) + mm(lo, second[0, rows, :]) + mm(hi, second[1, rows, :])
        col += n
        vh = v.astype(BF16).astype(F32)
        vl = v - vh
        for f in range(5):
            lhs_hi.append(dest[k * 5 + f] * vh[f : f + 1, :])
            lhs_lo.append(dest[k * 5 + f] * vl[f : f + 1, :])
    lhs = jnp.concatenate([jnp.concatenate(lhs_hi, axis=1), jnp.concatenate(lhs_lo, axis=1)], axis=0)
    image = lax.dot_general(
        lhs.astype(BF16), spots, (((1,), (1,)), ((), ())), preferred_element_type=F32
    )
    image = image[:16] + image[16:]
    sa[...] = image[:8]
    sb[...] = image[8:10]
    ga[0] = image[:8]
    gb[0] = image[8:10]
    ca = copies(sa, ga, y_peers, sem_as, sem_ar, 0)
    cb = copies(sb, gb, y_peers, sem_bs, sem_br, 0)
    for a, b in zip(ca, cb):
        a.start()
        b.start()

    nrow = ngy * 5
    q = iota((nrow, nlane), 0)
    lead = jnp.full((1, 1), agg[0], jnp.int32) == gy
    in_row = q - (starts >> 7)
    sel_a = jnp.where((in_row == iota((nrow, nlane), 1) % 8) & lead, 1.0, 0.0)
    q2 = iota((nrow, ngy * 2), 0)
    slot2 = iota((ngy, ngy * 2), 1) // 2
    before2 = jnp.where(turn(iota((ngy, ngy * 2), 0)) < turn(slot2), totals[:, : ngy * 2], 0.0)
    starts2 = jnp.sum(before2, axis=0, keepdims=True).astype(jnp.int32)
    sel_b = jnp.where((q2 - (starts2 >> 7) == 8 + iota((nrow, ngy * 2), 1) % 2) & lead, 1.0, 0.0)
    for a, b in zip(ca, cb):
        a.wait()
        b.wait()
    for k in range(ngy):
        gbrows[2 * k : 2 * k + 2, :] = gb[k]
    sel_a, sel_b = sel_a.astype(BF16), sel_b.astype(BF16)
    hi, lo = split(ga[...].reshape(ngy * 8, 128))
    hi2, lo2 = split(gbrows[...])
    snap_out[...] = (mm(sel_a, hi) + mm(sel_b, hi2)) + (mm(sel_a, lo) + mm(sel_b, lo2))


def shards(ngx, ngy, state, counts, aggregator):
    nx = INNER[ngx]
    nz = ngx // nx
    first, second, ranks, cmat = tables()
    vm = pltpu.VMEM
    dma = pltpu.SemaphoreType.DMA
    nmax = ngy + nz + nx
    vmem = pl.BlockSpec(memory_space=pltpu.VMEM)
    adv, snap = pl.pallas_call(
        functools.partial(kernel, ngx, ngy),
        out_shape=(
            vm((5, 8, 8, 128), F32),
            vm((ngy * 5, 128), F32),
        ),
        in_specs=[pl.BlockSpec(memory_space=pltpu.HBM)] * 7,
        out_specs=(vmem, vmem),
        scratch_shapes=[
            vm(state.shape, F32),
            vm(counts.shape, jnp.int32),
            pltpu.SMEM((1,), jnp.int32),
            vm(first.shape, BF16),
            vm(second.shape, BF16),
            vm(ranks.shape, jnp.int32),
            vm(cmat.shape, F32),
            dma((9,)),
            vm((5, 16, 8, 128), F32),
            vm((5, 12, 8, 128), F32),
            vm((5, 12, 8, 128), F32),
            vm((5, 12, 8, 128), F32),
            vm((5, 12, 8, 128), F32),
            vm((5, 12, 8, 128), F32),
            vm((5, 12, 8, 128), F32),
            vm((5, 8, 8, 128), F32),
            vm((5, 8, 8, 128), F32),
            vm((2, 5, 6, 8, 128), F32),
            vm((2, 5, 6, 8, 128), F32),
            vm((5, 8, 128), F32),
            vm((6, 5, 8, 128), F32),
            vm((2, 5, 2, 8, 128), F32),
            vm((3, 1, 128), F32),
            vm((ngy, 1, 128), F32),
            vm((nz, 1, 128), F32),
            vm((nx, 1, 128), F32),
            vm((ngy, 128), F32),
            vm((ngy, 8, 128), F32),
            vm((ngy, 2, 128), F32),
            vm((8, 128), F32),
            vm((2, 128), F32),
            vm((ngy * 2, 128), F32),
            vm((2, 5, 7, 8, 128), F32),
            vm((4, 5, 8, 128), F32),
            dma((2,)), dma((2,)), dma((6,)), dma((6,)), dma((nmax,)), dma((nmax,)),
            dma((ngy,)), dma((ngy,)), dma((ngy,)), dma((ngy,)),
        ],
        compiler_params=pltpu.CompilerParams(collective_id=0, has_side_effects=True),
        name="step",
    )(state, counts, aggregator, first, second, ranks, cmat)
    return adv, snap.reshape(1, 1, ngy * 640)


def solution(mesh):
    ngx, ngy = mesh.shape["gx"], mesh.shape["gy"]
    placed = (P(None, None, "gx", "gy"), P(None, None, "gx", "gy"), P("gx"))
    return jax.shard_map(
        functools.partial(shards, ngx, ngy),
        mesh=mesh,
        in_specs=placed,
        out_specs=(P(None, None, "gx", "gy"), P("gx", "gy", None)),
        check_vma=False,
    )
```

```python
import functools
import math

import jax
import jax.numpy as jnp
import numpy as np
from jax import lax
from jax.experimental import pallas as pl
from jax.experimental.pallas import tpu as pltpu
from jax.sharding import PartitionSpec as P

MESH = pl.DeviceIdType.MESH
F32 = jnp.float32
BF16 = jnp.bfloat16
GAMMA = 1.4
COURANT = 0.1
PAIR = 2
CORNERS = [(0, -1), (0, 1), (1, -1), (-1, -1), (1, 1), (-1, 1)]
CHUNKS = [[((0, 0), 4), ((0, 1), 3), ((0, 3), 1)], [((0, 2), 2), ((1, 0), 3), ((1, 1), 1), ((2, 0), 1)]]
COMBOS = [c for chunk in CHUNKS for c, _ in chunk]


def cosine_np():
    k = np.arange(8)[:, None]
    n = np.arange(8)[None, :]
    w = np.where(k == 0, math.sqrt(0.125), 0.5)
    return np.cos(math.pi * (2 * n + 1) * k / 16.0) * w


def rank_of():
    flat = np.arange(512)
    keys = (flat // 64 + flat // 8 % 8 + flat % 8) * 512 + flat
    order = np.argsort(keys, kind="stable")
    rank = np.empty(512, np.int64)
    rank[order] = np.arange(512)
    return rank.reshape(8, 8, 8)


def tables():
    c = cosine_np()
    rank = rank_of()
    first = np.zeros((56, 320), np.float32)
    for i, (kz, kx) in enumerate(COMBOS):
        for f in range(5):
            first[i * 8 + f, f * 64 : f * 64 + 64] = np.outer(c[kz], c[kx]).reshape(64)
    second = np.zeros((len(COMBOS) * 128, 128), np.float32)
    ranks = np.full((2, 128), 1000, np.int32)
    row = 0
    for k, chunk in enumerate(CHUNKS):
        slot = 0
        for (kz, kx), n in chunk:
            for ky in range(n):
                for b in range(16):
                    second[row * 128 + b * 8 : row * 128 + b * 8 + 8, slot * 16 + b] = c[ky]
                ranks[k, slot * 16 : slot * 16 + 16] = rank[kz, kx, ky]
                slot += 1
            row += 1
    b = np.arange(16)[:, None]
    lane = np.arange(128)[None, :] % 16
    count = np.concatenate([(b < lane), (b == lane), np.ones((16, 128))], axis=1).astype(np.float32)
    first_hi = first.astype(BF16)
    first_lo = (first - first_hi.astype(np.float32)).astype(BF16)
    second_hi = second.astype(BF16)
    second_lo = (second - second_hi.astype(np.float32)).astype(BF16)
    return np.concatenate([first_hi, first_lo]), np.stack([second_hi, second_lo]), ranks, count


def half_slope(a, b):
    return 0.5 * jnp.maximum(jnp.minimum(a, jnp.maximum(b, 0.0)), jnp.minimum(b, 0.0))


def prims_of(cons):
    rho, mx, my, mz, en = cons
    inv = 1.0 / rho
    u, v, w = mx * inv, my * inv, mz * inv
    p = (GAMMA - 1.0) * (en - 0.5 * (mx * u + my * v + mz * w))
    return [rho, u, v, w, p]


def root(x):
    return x * lax.rsqrt(jnp.maximum(x, 1e-37))


def flux2(left, right, comp):
    a = None
    for q in (left, right):
        s = jnp.abs(q[1 + comp]) + root(GAMMA * q[4] / q[0])
        a = s if a is None else jnp.maximum(a, s)
    out = None
    for q, away in ((left, None), (right, a)):
        rho, p, vel = q[0], q[4], q[1:4]
        vn = vel[comp]
        shift = vn + a if away is None else vn - a
        mass = rho * shift
        kin = 0.5 * (vel[0] * vel[0] + vel[1] * vel[1] + vel[2] * vel[2])
        rows = [mass] + [mass * v for v in vel]
        rows[1 + comp] = rows[1 + comp] + p
        rows.append(mass * kin + p * (shift * (1.0 / (GAMMA - 1.0)) + vn))
        out = rows if out is None else [x + y for x, y in zip(out, rows)]
    return out


def split(x):
    hi = x.astype(BF16)
    return hi, (x - hi.astype(F32)).astype(BF16)


def mm(a, b):
    return jnp.dot(a, b, preferred_element_type=F32)


def rollto(x, shift, axis):
    n = x.shape[axis]
    shift %= n
    return pltpu.roll(x, shift, axis) if shift else x


def last(x):
    return x.ndim - 1


def iota(shape, dim):
    return lax.broadcasted_iota(jnp.int32, shape, dim)


def z_term(w):
    out_l, out_r = [], []
    for x in w:
        d = x[1:] - x[:-1]
        h = half_slope(d[1:], d[:-1])
        c = x[1:-1]
        out_l.append((c + h)[:-1])
        out_r.append((c - h)[1:])
    f = flux2(out_l, out_r, 2)
    return [x[1:] - x[:-1] for x in f]


def x_next(a, b):
    row = iota(a.shape, a.ndim - 2)
    return jnp.where(row == 7, rollto(b, -1, b.ndim - 2), rollto(a, -1, a.ndim - 2))


def x_prev(a, b):
    row = iota(a.shape, a.ndim - 2)
    return jnp.where(row == 0, rollto(b, 1, b.ndim - 2), rollto(a, 1, a.ndim - 2))


def x_terms(a, b):
    la, ra, lb, rb = [], [], [], []
    for x, y in zip(a, b):
        fx, fy = x_next(x, y) - x, x_next(y, x) - y
        hx, hy = half_slope(fx, x_prev(fx, fy)), half_slope(fy, x_prev(fy, fx))
        la.append(x + hx)
        lb.append(y + hy)
        wx, wy = x - hx, y - hy
        ra.append(x_next(wx, wy))
        rb.append(x_next(wy, wx))
    fa, fb = flux2(la, ra, 0), flux2(lb, rb, 0)
    ta = [x - x_prev(x, y) for x, y in zip(fa, fb)]
    tb = [y - x_prev(y, x) for x, y in zip(fa, fb)]
    return ta, tb


def y_term(w, e1, e2):
    lane = iota(w[0].shape, last(w[0]))
    left, right = [], []
    for x, e, g in zip(w, e1, e2):
        nxt = jnp.where(lane == 127, e, rollto(x, -1, last(x)))
        prv = jnp.where(lane == 0, e, rollto(x, 1, last(x)))
        h = half_slope(nxt - x, x - prv)
        left.append(x + h)
        right.append(jnp.where(lane == 127, g, rollto(x - h, -1, last(x))))
    f = flux2(left, right, 1)
    return [x - jnp.where(lane == 0, g, rollto(x, 1, last(x))) for x, g in zip(f, e2)]


def packed_y(w):
    left, right = [], []
    for x in w:
        d = rollto(x, -1, last(x)) - x
        h = half_slope(d, rollto(d, 1, last(d)))
        left.append(x + h)
        right.append(x - h)
    f = flux2(left, [rollto(x, -1, last(x)) for x in right], 1)
    return right, f


def packed_z(w):
    left, right = [], []
    for x in w:
        d = rollto(x, -8, last(x)) - x
        h = half_slope(d, rollto(d, 8, last(d)))
        left.append(x + h)
        right.append(x - h)
    f = flux2(left, [rollto(x, -8, last(x)) for x in right], 2)
    return [x - rollto(x, 8, last(x)) for x in f]


def edge_lanes(low, high):
    col = iota(low.shape, last(low)) % 8
    return jnp.where(col == 7, rollto(high, 3, last(high)), rollto(low, 5, last(low)))


def pack_columns(planes, zs):
    out = None
    for z in zs:
        r = rollto(planes(z), 8 * z + 4, 1)
        out = r if out is None else jnp.where(iota(r.shape, 1) // 8 == z, r, out)
    return out


def kernel(
    ngx, ngy, state_in, counts_in, agg_in, first_in, second_in, ranks_in, cmat_in,
    adv, snap_out,
    state, counts, agg, first, second, ranks, cmat, sem_in,
    W, XH, L, Lx, Wx, E1, E2, E1x, E2x, sendx, recvx, qown, recvq, qx,
    maxsend, ry, rw, tot,
    ga, sa, xedge, xinj, pick,
    sem_h, sem_q, sem_y, sem_w, sem_a,
):
    loads = [
        pltpu.make_async_copy(src, dst, sem_in.at[i])
        for i, (src, dst) in enumerate(
            [(state_in.at[:, 4:12], state.at[:, 4:12]), (counts_in, counts), (cmat_in, cmat)]
            + [(state_in.at[:, 0:4], state.at[:, 0:4]), (state_in.at[:, 12:16], state.at[:, 12:16])]
            + [(agg_in, agg), (ranks_in, ranks), (first_in, first), (second_in, second)]
        )
    ]
    for c in loads:
        c.start()

    gx = lax.axis_index("gx")
    gy = lax.axis_index("gy")

    def at(dx, dy):
        x = lax.rem(gx + (dx % ngx), ngx) if dx else gx
        y = lax.rem(gy + (dy % ngy), ngy) if dy else gy
        return (x, y)

    y_peers = [at(0, k) for k in range(1, ngy)]
    w_peers = [at(k, 0) for k in range(1, ngx)]
    halo_peers = [at(-1, 0), at(1, 0)]
    q_peers = [at(-dx, -dy) for dx, dy in CORNERS]

    barrier = pltpu.get_barrier_semaphore()
    far_w = sorted(range(1, ngx), key=lambda k: abs(k - ngx // 2))
    far_y = sorted(range(1, ngy), key=lambda k: abs(k - ngy // 2))
    everyone = [w_peers[k - 1] for k in far_w] + [y_peers[k - 1] for k in far_y] + q_peers[2:]
    for peer in everyone:
        pl.semaphore_signal(barrier, inc=1, device_id=peer, device_id_type=MESH)

    for c in loads[:3]:
        c.wait()
    vmax = None
    for z in range(4, 12):
        w = prims_of([state[f, z] for f in range(5)])
        for f in range(5):
            W[f, z] = w[f]
        c = root(GAMMA * w[4] / w[0])
        s = jnp.maximum(jnp.maximum(jnp.abs(w[1]), jnp.abs(w[2])), jnp.abs(w[3])) + c
        vmax = s if vmax is None else jnp.maximum(vmax, s)
    top = jnp.max(jnp.max(vmax, axis=0, keepdims=True), axis=1, keepdims=True)

    cnt = jnp.zeros((8, 16), F32)
    row16 = iota((8, 16), 0)
    for f in range(5):
        cnt = jnp.where(row16 == f, counts[f, 0].astype(F32), cnt)
    cexp = jnp.dot(cnt, cmat[...], preferred_element_type=F32)
    total = jnp.sum(cexp[:, 256:384], axis=0, keepdims=True)
    lane1 = iota((1, 128), 1)
    maxsend[0] = jnp.where(lane1 < 64, top, total)
    ry[0] = maxsend[0]

    pl.semaphore_wait(barrier, len(everyone))

    def send(src, bufs, peers, order, sems):
        for k in order:
            pltpu.make_async_remote_copy(
                src_ref=src, dst_ref=bufs.at[k], send_sem=sems.at[0], recv_sem=sems.at[1],
                device_id=peers[k], device_id_type=MESH,
            ).start()

    def whole(ref, sems):
        return pltpu.make_async_remote_copy(
            src_ref=ref, dst_ref=ref, send_sem=sems.at[0], recv_sem=sems.at[1],
            device_id=y_peers[0], device_id_type=MESH,
        )

    y_of = dict(zip(range(1, ngy), y_peers))
    w_of = dict(zip(range(1, ngx), w_peers))
    all_y, all_w = whole(ry.at[pl.ds(1, ngy - 1)], sem_y), whole(rw.at[pl.ds(1, ngx - 1)], sem_w)
    all_q, all_h = whole(recvq, sem_q), whole(recvx, sem_h)
    all_a = whole(ga.at[pl.ds(1, ngy - 1), pl.ds(0, 10)], sem_a)
    send(maxsend.at[0], ry, y_of, far_y, sem_y)
    for c in loads[3:]:
        c.wait()
    row8 = iota((8, 128), 0)
    for f in range(5):
        for k in range(6):
            lo, hi = state[f, 2 + k], state[f, 8 + k]
            sendx[0, f, k] = jnp.where(row8 < 4, lo, rollto(hi, 4, 0))
            sendx[1, f, k] = jnp.where(row8 < 4, rollto(lo, 4, 0), hi)
        qown[f] = pack_columns(lambda z: state[f, z], range(16))
    send(qown, recvq, q_peers, range(6), sem_q)
    for i, peer in enumerate(halo_peers):
        pltpu.make_async_remote_copy(
            src_ref=sendx.at[i], dst_ref=recvx.at[i], send_sem=sem_h.at[0], recv_sem=sem_h.at[1],
            device_id=peer, device_id_type=MESH,
        ).start()
    for z in (*range(0, 4), *range(12, 16)):
        w = prims_of([state[f, z] for f in range(5)])
        for f in range(5):
            W[f, z] = w[f]

    def load(ref, start, n):
        return [ref[f, pl.ds(start, n)] for f in range(5)]

    def z_main(i, carry):
        z0 = i * PAIR
        t = z_term(load(W, z0, PAIR + 4))
        for f in range(5):
            L[f, pl.ds(z0, PAIR)] = t[f]
        return carry

    lax.fori_loop(0, 12 // PAIR, z_main, 0)

    all_y.wait_recv()
    best = ry[0]
    for k in range(ngy):
        if k:
            best = jnp.maximum(best, ry[k])
        tot[k : k + 1, :] = jnp.where(lane1 < 64, rollto(ry[k], 64, 1), ry[k])
    maxsend[1] = jnp.where(lane1 < 64, best, rollto(best, 64, 1))
    send(maxsend.at[1], rw, w_of, far_w, sem_w)

    all_q.wait_recv()
    all_h.wait_recv()
    for f in range(5):
        for k in range(6):
            a, b = recvx[0, f, k], recvx[1, f, k]
            XH[f, k] = jnp.where(row8 < 4, a, rollto(b, 4, 0))
            XH[f, k + 6] = jnp.where(row8 < 4, rollto(a, 4, 0), b)
    for z in range(12):
        w = prims_of([XH[f, z] for f in range(5)])
        for f in range(5):
            Wx[f, z] = w[f]
    colm = iota((8, 128), 1) % 8
    packed = []
    for f in range(5):
        q = qown[f]
        qh = pack_columns(lambda z: XH[f, z - 2], range(2, 14))
        lo = jnp.where(row8 < 4, recvq[2, f], recvq[3, f])
        hi = jnp.where(row8 < 4, recvq[4, f], recvq[5, f])
        packed.append(
            jnp.stack(
                [
                    jnp.where(colm < 4, recvq[0, f], q),
                    jnp.where(colm < 4, q, recvq[1, f]),
                    jnp.where(colm < 4, lo, qh),
                    jnp.where(colm < 4, qh, hi),
                ]
            )
        )
    pw = prims_of(packed)
    pr, pf = packed_y(pw)
    ta, _ = x_terms([x[:2] for x in pw], [x[2:] for x in pw])
    tz = packed_z([x[:2] for x in pw])
    for f in range(5):
        ty = pf[f] - rollto(pf[f], 1, 2)
        qx[0, f] = packed[f][:2]
        qx[1, f] = ta[f] + tz[f] + ty[:2]

    def inject(e1, e2, pw, pr, pf, low, high, planes, offset):
        for f in range(5):
            c1 = edge_lanes(pw[f][low], pw[f][high])
            c2 = edge_lanes(pf[f][low], pr[f][high])
            for z in planes:
                e1[f, z - offset] = rollto(c1, -(8 * z + 8), 1)
                e2[f, z - offset] = rollto(c2, -(8 * z + 8), 1)

    inject(E1, E2, pw, pr, pf, 0, 1, range(2, 14), 2)
    inject(E1x, E2x, pw, pr, pf, 2, 3, range(4, 12), 4)

    def xy_main(i, carry):
        z0 = i * PAIR
        a = load(W, z0 + 2, PAIR)
        ta, tb = x_terms(a, load(Wx, z0, PAIR))
        ty = y_term(a, load(E1, z0, PAIR), load(E2, z0, PAIR))
        for f in range(5):
            L[f, pl.ds(z0, PAIR)] = L[f, pl.ds(z0, PAIR)] + ta[f] + ty[f]
            Lx[f, pl.ds(z0, PAIR)] = tb[f]
        return carry

    lax.fori_loop(0, 12 // PAIR, xy_main, 0)

    def strip(i, carry):
        z0 = i * PAIR
        w = load(Wx, z0, PAIR + 4)
        tz = z_term(w)
        ty = y_term([x[2:-2] for x in w], load(E1x, z0, PAIR), load(E2x, z0, PAIR))
        for f in range(5):
            Lx[f, pl.ds(z0 + 2, PAIR)] = Lx[f, pl.ds(z0 + 2, PAIR)] + tz[f] + ty[f]
        return carry

    lax.fori_loop(0, 8 // PAIR, strip, 0)
    for f in range(5):
        for j, r in enumerate((6, 7, 0, 1)):
            for z in range(8):
                xedge[0, f, j, z : z + 1, :] = XH[f, z + 2, r : r + 1, :]
                xedge[1, f, j, z : z + 1, :] = Lx[f, z + 2, r : r + 1, :]
        for j, r in enumerate((0, 1, 7)):
            for z in range(8):
                xedge[0, f, j + 4, z : z + 1, :] = state[f, z + 4, r : r + 1, :]
                xedge[1, f, j + 4, z : z + 1, :] = L[f, z + 2, r : r + 1, :]

    leader = agg[...]
    me_rank = (gy - leader + ngy) & (ngy - 1)
    nlane = ngy * 16
    slot_col = iota((ngy, nlane), 0)
    slot_row = iota((ngy, nlane), 1) // 16

    def turn(slot):
        return (gy - slot - leader + 2 * ngy) & (ngy - 1)

    totals = tot[...]
    wide = jnp.broadcast_to(totals[:, :1], (ngy, nlane))
    before = jnp.where(turn(slot_col) < turn(slot_row), wide, 0.0)
    starts = jnp.sum(before, axis=0, keepdims=True).astype(jnp.int32)
    mine = jnp.sum(
        jnp.where(turn(iota((ngy, 128), 0)) < me_rank, totals, 0.0), axis=0, keepdims=True
    ).astype(jnp.int32)
    field_total = cexp[:, 256:384]
    upto = cexp[:, :128]
    for f in range(4):
        upto = upto + jnp.where(row8 > f, field_total[f : f + 1, :], 0.0)
    own_count = cexp[:, 128:256].astype(jnp.int32)
    base = upto.astype(jnp.int32) + (mine & 127)
    dest, spots = [], []
    for k in range(2):
        rank = ranks[k : k + 1, :]
        pos = base + rank
        keep = rank < own_count
        row_to = jnp.where(keep, pos >> 7, -1)
        lane_to = pos & 127
        for f in range(5):
            dest.append(row_to[f : f + 1, :])
            spots.append((iota((128, 128), 0) == lane_to[f : f + 1, :]).astype(F32).astype(BF16))
    spots = jnp.concatenate(spots, axis=1)
    dest = [(iota((16, 128), 0) == d).astype(F32) for d in dest]

    nrow = ngy * 5
    q = iota((nrow, nlane), 0)
    lead = me_rank == 0
    in_row = q - (starts >> 7)
    pick[...] = jnp.where((in_row == iota((nrow, nlane), 1) % 16) & lead, 1.0, 0.0).astype(BF16)
    ga[:, 10:16] = jnp.zeros((ngy, 6, 128), F32)

    all_w.wait_recv()
    best = maxsend[1]
    for k in range(1, ngx):
        best = jnp.maximum(best, rw[k])
    ratio = COURANT / best
    half = -0.5 * ratio

    p1 = prims_of([qx[0, f] + half * qx[1, f] for f in range(5)])
    pr, pf = packed_y(p1)
    inject(E1, E2, p1, pr, pf, 0, 1, range(4, 12), 4)
    we = prims_of([xedge[0, f] + half * xedge[1, f] for f in range(5)])
    fl, fr = [], []
    for f in range(5):
        m2, m1, p8, p9, c0, c1, c7 = [we[f][j] for j in range(7)]
        h = half_slope(c0 - m1, m1 - m2)
        g = half_slope(c1 - c0, c0 - m1)
        fl.append(m1 + h)
        fr.append(c0 - g)
        xinj[0, f] = m1
        xinj[1, f] = p8
        xinj[2, f] = p8 - half_slope(p9 - p8, p8 - c7)
    fx = flux2(fl, fr, 0)
    for f in range(5):
        xinj[3, f] = fx[f]

    for z in range(12):
        s = [state[f, z + 2] + half * L[f, z] for f in range(5)]
        w = prims_of(s)
        for f in range(5):
            L[f, z] = s[f]
            W[f, z] = w[f]

    for z0 in range(0, 8, PAIR):
        w = load(W, z0, PAIR + 4)
        tz = z_term(w)
        c = [x[2:-2] for x in w]
        ty = y_term(c, load(E1, z0, PAIR), load(E2, z0, PAIR))

        def rows(j, f, z0=z0):
            return jnp.stack([xinj[j, f, pl.ds(z0 + d, 1), :] for d in range(PAIR)])

        row = iota(c[0].shape, 1)
        left, right, inj = [], [], []
        for f in range(5):
            x = c[f]
            nxt = jnp.where(row == 7, rows(1, f), rollto(x, -1, 1))
            prv = jnp.where(row == 0, rows(0, f), rollto(x, 1, 1))
            h = half_slope(nxt - x, x - prv)
            left.append(x + h)
            right.append(jnp.where(row == 7, rows(2, f), rollto(x - h, -1, 1)))
        fx = flux2(left, right, 0)
        for f in range(5):
            tx = fx[f] - jnp.where(row == 0, rows(3, f), rollto(fx[f], 1, 1))
            s = L[f, pl.ds(z0 + 2, PAIR)] + half * (tx + ty[f] + tz[f])
            adv[f, pl.ds(z0, PAIR)] = 0.5 * state[f, pl.ds(z0 + 4, PAIR)] + 0.5 * s


    hi, lo = split(adv[...].reshape(320, 128))
    y1 = mm(first[...], hi)
    y1 = y1[:56] + y1[56:] + mm(first[:56, :], lo)
    col = 0
    lhs_hi, lhs_lo = [], []
    for k, chunk in enumerate(CHUNKS):
        n = len(chunk)
        y2 = jnp.concatenate([y1[(col + i) * 8 : (col + i) * 8 + 8] for i in range(n)], axis=1)
        hi, lo = split(y2)
        rows = slice(col * 128, (col + n) * 128)
        v = mm(hi, second[0, rows, :]) + mm(lo, second[0, rows, :]) + mm(hi, second[1, rows, :])
        col += n
        vh = v.astype(BF16).astype(F32)
        vl = v - vh
        for f in range(5):
            lhs_hi.append(dest[k * 5 + f] * vh[f : f + 1, :])
            lhs_lo.append(dest[k * 5 + f] * vl[f : f + 1, :])
    lhs = jnp.concatenate([jnp.concatenate(lhs_hi, axis=1), jnp.concatenate(lhs_lo, axis=1)], axis=0)
    image = lax.dot_general(
        lhs.astype(BF16), spots, (((1,), (1,)), ((), ())), preferred_element_type=F32
    )
    image = image[:16] + image[16:]
    sa[...] = image
    ga[0] = image
    send(sa.at[pl.ds(0, 10)], ga.at[:, pl.ds(0, 10)], y_of, far_y, sem_a)

    for c in (all_y, all_w, all_q, all_h):
        c.wait_send()
    all_a.wait()
    hi, lo = split(ga[...].reshape(ngy * 16, 128))
    snap_out[...] = mm(pick[...], hi) + mm(pick[...], lo)


def shards(ngx, ngy, state, counts, aggregator):
    first, second, ranks, cmat = tables()
    vm = pltpu.VMEM
    dma = pltpu.SemaphoreType.DMA
    vmem = pl.BlockSpec(memory_space=pltpu.VMEM)
    adv, snap = pl.pallas_call(
        functools.partial(kernel, ngx, ngy),
        out_shape=(
            vm((5, 8, 8, 128), F32),
            vm((ngy * 5, 128), F32),
        ),
        in_specs=[pl.BlockSpec(memory_space=pltpu.HBM)] * 7,
        out_specs=(vmem, vmem),
        scratch_shapes=[
            vm(state.shape, F32),
            vm(counts.shape, jnp.int32),
            vm((1, 1), jnp.int32),
            vm(first.shape, BF16),
            vm(second.shape, BF16),
            vm(ranks.shape, jnp.int32),
            vm(cmat.shape, F32),
            dma((9,)),
            vm((5, 16, 8, 128), F32),
            vm((5, 12, 8, 128), F32),
            vm((5, 12, 8, 128), F32),
            vm((5, 12, 8, 128), F32),
            vm((5, 12, 8, 128), F32),
            vm((5, 12, 8, 128), F32),
            vm((5, 12, 8, 128), F32),
            vm((5, 8, 8, 128), F32),
            vm((5, 8, 8, 128), F32),
            vm((2, 5, 6, 8, 128), F32),
            vm((2, 5, 6, 8, 128), F32),
            vm((5, 8, 128), F32),
            vm((6, 5, 8, 128), F32),
            vm((2, 5, 2, 8, 128), F32),
            vm((2, 1, 128), F32),
            vm((ngy, 1, 128), F32),
            vm((ngx, 1, 128), F32),
            vm((ngy, 128), F32),
            vm((ngy, 16, 128), F32),
            vm((16, 128), F32),
            vm((2, 5, 7, 8, 128), F32),
            vm((4, 5, 8, 128), F32),
            vm((ngy * 5, ngy * 16), BF16),
            dma((2,)), dma((2,)), dma((2,)), dma((2,)), dma((2,)),
        ],
        compiler_params=pltpu.CompilerParams(collective_id=0, has_side_effects=True),
        name="step",
    )(state, counts, aggregator.reshape(1, 1), first, second, ranks, cmat)
    return adv, snap.reshape(1, 1, ngy * 640)


def solution(mesh):
    ngx, ngy = mesh.shape["gx"], mesh.shape["gy"]
    placed = (P(None, None, "gx", "gy"), P(None, None, "gx", "gy"), P("gx"))
    return jax.shard_map(
        functools.partial(shards, ngx, ngy),
        mesh=mesh,
        in_specs=placed,
        out_specs=(P(None, None, "gx", "gy"), P("gx", "gy", None)),
        check_vma=False,
    )
```

```python
import functools
import math

import jax
import jax.numpy as jnp
import numpy as np
from jax import lax
from jax.experimental import pallas as pl
from jax.experimental.pallas import tpu as pltpu
from jax.sharding import PartitionSpec as P

MESH = pl.DeviceIdType.MESH
F32 = jnp.float32
BF16 = jnp.bfloat16
GAMMA = 1.4
COURANT = 0.1
PAIR = 2
CORNERS = [(0, -1), (0, 1), (1, -1), (-1, -1), (1, 1), (-1, 1)]
CHUNKS = [[((0, 0), 4), ((0, 1), 3), ((0, 3), 1)], [((0, 2), 2), ((1, 0), 3), ((1, 1), 1), ((2, 0), 1)]]
COMBOS = [c for chunk in CHUNKS for c, _ in chunk]


def cosine_np():
    k = np.arange(8)[:, None]
    n = np.arange(8)[None, :]
    w = np.where(k == 0, math.sqrt(0.125), 0.5)
    return np.cos(math.pi * (2 * n + 1) * k / 16.0) * w


def rank_of():
    flat = np.arange(512)
    keys = (flat // 64 + flat // 8 % 8 + flat % 8) * 512 + flat
    order = np.argsort(keys, kind="stable")
    rank = np.empty(512, np.int64)
    rank[order] = np.arange(512)
    return rank.reshape(8, 8, 8)


def tables():
    c = cosine_np()
    rank = rank_of()
    first = np.zeros((56, 320), np.float32)
    for i, (kz, kx) in enumerate(COMBOS):
        for f in range(5):
            first[i * 8 + f, f * 64 : f * 64 + 64] = np.outer(c[kz], c[kx]).reshape(64)
    second = np.zeros((len(COMBOS) * 128, 128), np.float32)
    ranks = np.full((2, 128), 1000, np.int32)
    row = 0
    for k, chunk in enumerate(CHUNKS):
        slot = 0
        for (kz, kx), n in chunk:
            for ky in range(n):
                for b in range(16):
                    second[row * 128 + b * 8 : row * 128 + b * 8 + 8, slot * 16 + b] = c[ky]
                ranks[k, slot * 16 : slot * 16 + 16] = rank[kz, kx, ky]
                slot += 1
            row += 1
    b = np.arange(16)[:, None]
    lane = np.arange(128)[None, :] % 16
    count = np.concatenate([(b < lane), (b == lane), np.ones((16, 128))], axis=1).astype(np.float32)
    first_hi = first.astype(BF16)
    first_lo = (first - first_hi.astype(np.float32)).astype(BF16)
    second_hi = second.astype(BF16)
    second_lo = (second - second_hi.astype(np.float32)).astype(BF16)
    return np.concatenate([first_hi, first_lo]), np.stack([second_hi, second_lo]), ranks, count


def half_slope(a, b):
    return 0.5 * jnp.maximum(jnp.minimum(a, jnp.maximum(b, 0.0)), jnp.minimum(b, 0.0))


def prims_of(cons):
    rho, mx, my, mz, en = cons
    inv = 1.0 / rho
    u, v, w = mx * inv, my * inv, mz * inv
    p = (GAMMA - 1.0) * (en - 0.5 * (mx * u + my * v + mz * w))
    return [rho, u, v, w, p]


def root(x):
    return x * lax.rsqrt(jnp.maximum(x, 1e-37))


def flux2(left, right, comp):
    a = None
    for q in (left, right):
        s = jnp.abs(q[1 + comp]) + root(GAMMA * q[4] / q[0])
        a = s if a is None else jnp.maximum(a, s)
    out = None
    for q, away in ((left, None), (right, a)):
        rho, p, vel = q[0], q[4], q[1:4]
        vn = vel[comp]
        shift = vn + a if away is None else vn - a
        mass = rho * shift
        kin = 0.5 * (vel[0] * vel[0] + vel[1] * vel[1] + vel[2] * vel[2])
        rows = [mass] + [mass * v for v in vel]
        rows[1 + comp] = rows[1 + comp] + p
        rows.append(mass * kin + p * (shift * (1.0 / (GAMMA - 1.0)) + vn))
        out = rows if out is None else [x + y for x, y in zip(out, rows)]
    return out


def split(x):
    hi = x.astype(BF16)
    return hi, (x - hi.astype(F32)).astype(BF16)


def mm(a, b):
    return jnp.dot(a, b, preferred_element_type=F32)


def rollto(x, shift, axis):
    n = x.shape[axis]
    shift %= n
    return pltpu.roll(x, shift, axis) if shift else x


def last(x):
    return x.ndim - 1


def iota(shape, dim):
    return lax.broadcasted_iota(jnp.int32, shape, dim)


def z_term(w):
    out_l, out_r = [], []
    for x in w:
        d = x[1:] - x[:-1]
        h = half_slope(d[1:], d[:-1])
        c = x[1:-1]
        out_l.append((c + h)[:-1])
        out_r.append((c - h)[1:])
    f = flux2(out_l, out_r, 2)
    return [x[1:] - x[:-1] for x in f]


def x_next(a, b):
    row = iota(a.shape, a.ndim - 2)
    return jnp.where(row == 7, rollto(b, -1, b.ndim - 2), rollto(a, -1, a.ndim - 2))


def x_prev(a, b):
    row = iota(a.shape, a.ndim - 2)
    return jnp.where(row == 0, rollto(b, 1, b.ndim - 2), rollto(a, 1, a.ndim - 2))


def x_terms(a, b):
    la, ra, lb, rb = [], [], [], []
    for x, y in zip(a, b):
        fx, fy = x_next(x, y) - x, x_next(y, x) - y
        hx, hy = half_slope(fx, x_prev(fx, fy)), half_slope(fy, x_prev(fy, fx))
        la.append(x + hx)
        lb.append(y + hy)
        wx, wy = x - hx, y - hy
        ra.append(x_next(wx, wy))
        rb.append(x_next(wy, wx))
    fa, fb = flux2(la, ra, 0), flux2(lb, rb, 0)
    ta = [x - x_prev(x, y) for x, y in zip(fa, fb)]
    tb = [y - x_prev(y, x) for x, y in zip(fa, fb)]
    return ta, tb


def y_term(w, e1, e2):
    lane = iota(w[0].shape, last(w[0]))
    left, right = [], []
    for x, e, g in zip(w, e1, e2):
        nxt = jnp.where(lane == 127, e, rollto(x, -1, last(x)))
        prv = jnp.where(lane == 0, e, rollto(x, 1, last(x)))
        h = half_slope(nxt - x, x - prv)
        left.append(x + h)
        right.append(jnp.where(lane == 127, g, rollto(x - h, -1, last(x))))
    f = flux2(left, right, 1)
    return [x - jnp.where(lane == 0, g, rollto(x, 1, last(x))) for x, g in zip(f, e2)]


def packed_y(w):
    left, right = [], []
    for x in w:
        d = rollto(x, -1, last(x)) - x
        h = half_slope(d, rollto(d, 1, last(d)))
        left.append(x + h)
        right.append(x - h)
    f = flux2(left, [rollto(x, -1, last(x)) for x in right], 1)
    return right, f


def packed_z(w):
    left, right = [], []
    for x in w:
        d = rollto(x, -8, last(x)) - x
        h = half_slope(d, rollto(d, 8, last(d)))
        left.append(x + h)
        right.append(x - h)
    f = flux2(left, [rollto(x, -8, last(x)) for x in right], 2)
    return [x - rollto(x, 8, last(x)) for x in f]


def edge_lanes(low, high):
    col = iota(low.shape, last(low)) % 8
    return jnp.where(col == 7, rollto(high, 3, last(high)), rollto(low, 5, last(low)))


def pack_columns(planes, zs):
    out = None
    for z in zs:
        r = rollto(planes(z), 8 * z + 4, 1)
        out = r if out is None else jnp.where(iota(r.shape, 1) // 8 == z, r, out)
    return out


def kernel(
    ngx, ngy, state_in, counts_in, agg_in, first_in, second_in, ranks_in, cmat_in,
    adv, ga, pick,
    state, counts, agg, first, second, ranks, cmat, sem_in,
    W, XH, L, Lx, Wx, E1, E2, E1x, E2x, sendx, recvx, qown, recvq, qx,
    maxsend, ry, rw, tot,
    sa, xedge, xinj,
    sem_h, sem_q, sem_y, sem_w, sem_a,
):
    loads = [
        pltpu.make_async_copy(src, dst, sem_in.at[i])
        for i, (src, dst) in enumerate(
            [(state_in.at[:, 4:12], state.at[:, 4:12]), (counts_in, counts), (cmat_in, cmat)]
            + [(state_in.at[:, 0:4], state.at[:, 0:4]), (state_in.at[:, 12:16], state.at[:, 12:16])]
            + [(agg_in, agg), (ranks_in, ranks), (first_in, first), (second_in, second)]
        )
    ]
    for c in loads:
        c.start()

    gx = lax.axis_index("gx")
    gy = lax.axis_index("gy")

    def at(dx, dy):
        x = lax.rem(gx + (dx % ngx), ngx) if dx else gx
        y = lax.rem(gy + (dy % ngy), ngy) if dy else gy
        return (x, y)

    y_peers = [at(0, k) for k in range(1, ngy)]
    w_peers = [at(k, 0) for k in range(1, ngx)]
    halo_peers = [at(-1, 0), at(1, 0)]
    q_peers = [at(-dx, -dy) for dx, dy in CORNERS]

    barrier = pltpu.get_barrier_semaphore()
    far_w = sorted(range(1, ngx), key=lambda k: abs(k - ngx // 2))
    far_y = sorted(range(1, ngy), key=lambda k: abs(k - ngy // 2))
    everyone = [w_peers[k - 1] for k in far_w] + [y_peers[k - 1] for k in far_y] + q_peers[2:]
    for peer in everyone:
        pl.semaphore_signal(barrier, inc=1, device_id=peer, device_id_type=MESH)

    for c in loads[:3]:
        c.wait()
    vmax = None
    for z in range(4, 12):
        w = prims_of([state[f, z] for f in range(5)])
        for f in range(5):
            W[f, z] = w[f]
        c = root(GAMMA * w[4] / w[0])
        s = jnp.maximum(jnp.maximum(jnp.abs(w[1]), jnp.abs(w[2])), jnp.abs(w[3])) + c
        vmax = s if vmax is None else jnp.maximum(vmax, s)
    top = jnp.max(jnp.max(vmax, axis=0, keepdims=True), axis=1, keepdims=True)

    cnt = jnp.zeros((8, 16), F32)
    row16 = iota((8, 16), 0)
    for f in range(5):
        cnt = jnp.where(row16 == f, counts[f, 0].astype(F32), cnt)
    cexp = jnp.dot(cnt, cmat[...], preferred_element_type=F32)
    total = jnp.sum(cexp[:, 256:384], axis=0, keepdims=True)
    lane1 = iota((1, 128), 1)
    maxsend[0] = jnp.where(lane1 < 64, top, total)
    ry[0] = maxsend[0]

    pl.semaphore_wait(barrier, len(everyone))

    def send(src, bufs, peers, order, sems):
        for k in order:
            pltpu.make_async_remote_copy(
                src_ref=src, dst_ref=bufs.at[k], send_sem=sems.at[0], recv_sem=sems.at[1],
                device_id=peers[k], device_id_type=MESH,
            ).start()

    def whole(ref, sems):
        return pltpu.make_async_remote_copy(
            src_ref=ref, dst_ref=ref, send_sem=sems.at[0], recv_sem=sems.at[1],
            device_id=y_peers[0], device_id_type=MESH,
        )

    y_of = dict(zip(range(1, ngy), y_peers))
    w_of = dict(zip(range(1, ngx), w_peers))
    all_y, all_w = whole(ry.at[pl.ds(1, ngy - 1)], sem_y), whole(rw.at[pl.ds(1, ngx - 1)], sem_w)
    all_q, all_h = whole(recvq, sem_q), whole(recvx, sem_h)
    all_a = whole(ga.at[pl.ds(1, ngy - 1), pl.ds(0, 10)], sem_a)
    send(maxsend.at[0], ry, y_of, far_y, sem_y)
    for c in loads[3:]:
        c.wait()
    row8 = iota((8, 128), 0)
    for f in range(5):
        for k in range(6):
            lo, hi = state[f, 2 + k], state[f, 8 + k]
            sendx[0, f, k] = jnp.where(row8 < 4, lo, rollto(hi, 4, 0))
            sendx[1, f, k] = jnp.where(row8 < 4, rollto(lo, 4, 0), hi)
        qown[f] = pack_columns(lambda z: state[f, z], range(16))
    send(qown, recvq, q_peers, range(6), sem_q)
    for i, peer in enumerate(halo_peers):
        pltpu.make_async_remote_copy(
            src_ref=sendx.at[i], dst_ref=recvx.at[i], send_sem=sem_h.at[0], recv_sem=sem_h.at[1],
            device_id=peer, device_id_type=MESH,
        ).start()
    for z in (*range(0, 4), *range(12, 16)):
        w = prims_of([state[f, z] for f in range(5)])
        for f in range(5):
            W[f, z] = w[f]

    def load(ref, start, n):
        return [ref[f, pl.ds(start, n)] for f in range(5)]

    def z_main(i, carry):
        z0 = i * PAIR
        t = z_term(load(W, z0, PAIR + 4))
        for f in range(5):
            L[f, pl.ds(z0, PAIR)] = t[f]
        return carry

    lax.fori_loop(0, 12 // PAIR, z_main, 0)

    all_y.wait_recv()
    best = ry[0]
    for k in range(ngy):
        if k:
            best = jnp.maximum(best, ry[k])
        tot[k : k + 1, :] = jnp.where(lane1 < 64, rollto(ry[k], 64, 1), ry[k])
    maxsend[1] = jnp.where(lane1 < 64, best, rollto(best, 64, 1))
    send(maxsend.at[1], rw, w_of, far_w, sem_w)

    all_q.wait_recv()
    all_h.wait_recv()
    for f in range(5):
        for k in range(6):
            a, b = recvx[0, f, k], recvx[1, f, k]
            XH[f, k] = jnp.where(row8 < 4, a, rollto(b, 4, 0))
            XH[f, k + 6] = jnp.where(row8 < 4, rollto(a, 4, 0), b)
    for z in range(12):
        w = prims_of([XH[f, z] for f in range(5)])
        for f in range(5):
            Wx[f, z] = w[f]
    colm = iota((8, 128), 1) % 8
    packed = []
    for f in range(5):
        q = qown[f]
        qh = pack_columns(lambda z: XH[f, z - 2], range(2, 14))
        lo = jnp.where(row8 < 4, recvq[2, f], recvq[3, f])
        hi = jnp.where(row8 < 4, recvq[4, f], recvq[5, f])
        packed.append(
            jnp.stack(
                [
                    jnp.where(colm < 4, recvq[0, f], q),
                    jnp.where(colm < 4, q, recvq[1, f]),
                    jnp.where(colm < 4, lo, qh),
                    jnp.where(colm < 4, qh, hi),
                ]
            )
        )
    pw = prims_of(packed)
    pr, pf = packed_y(pw)
    ta, _ = x_terms([x[:2] for x in pw], [x[2:] for x in pw])
    tz = packed_z([x[:2] for x in pw])
    for f in range(5):
        ty = pf[f] - rollto(pf[f], 1, 2)
        qx[0, f] = packed[f][:2]
        qx[1, f] = ta[f] + tz[f] + ty[:2]

    def inject(e1, e2, pw, pr, pf, low, high, planes, offset):
        for f in range(5):
            c1 = edge_lanes(pw[f][low], pw[f][high])
            c2 = edge_lanes(pf[f][low], pr[f][high])
            for z in planes:
                e1[f, z - offset] = rollto(c1, -(8 * z + 8), 1)
                e2[f, z - offset] = rollto(c2, -(8 * z + 8), 1)

    inject(E1, E2, pw, pr, pf, 0, 1, range(2, 14), 2)
    inject(E1x, E2x, pw, pr, pf, 2, 3, range(4, 12), 4)

    def xy_main(i, carry):
        z0 = i * PAIR
        a = load(W, z0 + 2, PAIR)
        ta, tb = x_terms(a, load(Wx, z0, PAIR))
        ty = y_term(a, load(E1, z0, PAIR), load(E2, z0, PAIR))
        for f in range(5):
            L[f, pl.ds(z0, PAIR)] = L[f, pl.ds(z0, PAIR)] + ta[f] + ty[f]
            Lx[f, pl.ds(z0, PAIR)] = tb[f]
        return carry

    lax.fori_loop(0, 12 // PAIR, xy_main, 0)

    def strip(i, carry):
        z0 = i * PAIR
        w = load(Wx, z0, PAIR + 4)
        tz = z_term(w)
        ty = y_term([x[2:-2] for x in w], load(E1x, z0, PAIR), load(E2x, z0, PAIR))
        for f in range(5):
            Lx[f, pl.ds(z0 + 2, PAIR)] = Lx[f, pl.ds(z0 + 2, PAIR)] + tz[f] + ty[f]
        return carry

    lax.fori_loop(0, 8 // PAIR, strip, 0)
    for f in range(5):
        for j, r in enumerate((6, 7, 0, 1)):
            for z in range(8):
                xedge[0, f, j, z : z + 1, :] = XH[f, z + 2, r : r + 1, :]
                xedge[1, f, j, z : z + 1, :] = Lx[f, z + 2, r : r + 1, :]
        for j, r in enumerate((0, 1, 7)):
            for z in range(8):
                xedge[0, f, j + 4, z : z + 1, :] = state[f, z + 4, r : r + 1, :]
                xedge[1, f, j + 4, z : z + 1, :] = L[f, z + 2, r : r + 1, :]

    leader = agg[...]
    me_rank = (gy - leader + ngy) & (ngy - 1)
    nlane = ngy * 16
    slot_col = iota((ngy, nlane), 0)
    slot_row = iota((ngy, nlane), 1) // 16

    def turn(slot):
        return (gy - slot - leader + 2 * ngy) & (ngy - 1)

    totals = tot[...]
    wide = jnp.broadcast_to(totals[:, :1], (ngy, nlane))
    before = jnp.where(turn(slot_col) < turn(slot_row), wide, 0.0)
    starts = jnp.sum(before, axis=0, keepdims=True).astype(jnp.int32)
    mine = jnp.sum(
        jnp.where(turn(iota((ngy, 128), 0)) < me_rank, totals, 0.0), axis=0, keepdims=True
    ).astype(jnp.int32)
    field_total = cexp[:, 256:384]
    upto = cexp[:, :128]
    for f in range(4):
        upto = upto + jnp.where(row8 > f, field_total[f : f + 1, :], 0.0)
    own_count = cexp[:, 128:256].astype(jnp.int32)
    base = upto.astype(jnp.int32) + (mine & 127)
    dest, spots = [], []
    for k in range(2):
        rank = ranks[k : k + 1, :]
        pos = base + rank
        keep = rank < own_count
        row_to = jnp.where(keep, pos >> 7, -1)
        lane_to = pos & 127
        for f in range(5):
            dest.append(row_to[f : f + 1, :])
            spots.append((iota((128, 128), 0) == lane_to[f : f + 1, :]).astype(F32).astype(BF16))
    spots = jnp.concatenate(spots, axis=1)
    dest = [(iota((16, 128), 0) == d).astype(F32) for d in dest]

    nrow = ngy * 5
    q = iota((nrow, nlane), 0)
    lead = me_rank == 0
    in_row = q - (starts >> 7)
    pick[...] = jnp.where((in_row == iota((nrow, nlane), 1) % 16) & lead, 1.0, 0.0).astype(BF16)
    ga[:, 10:16] = jnp.zeros((ngy, 6, 128), F32)

    all_w.wait_recv()
    best = maxsend[1]
    for k in range(1, ngx):
        best = jnp.maximum(best, rw[k])
    ratio = COURANT / best
    half = -0.5 * ratio

    p1 = prims_of([qx[0, f] + half * qx[1, f] for f in range(5)])
    pr, pf = packed_y(p1)
    inject(E1, E2, p1, pr, pf, 0, 1, range(4, 12), 4)
    we = prims_of([xedge[0, f] + half * xedge[1, f] for f in range(5)])
    fl, fr = [], []
    for f in range(5):
        m2, m1, p8, p9, c0, c1, c7 = [we[f][j] for j in range(7)]
        h = half_slope(c0 - m1, m1 - m2)
        g = half_slope(c1 - c0, c0 - m1)
        fl.append(m1 + h)
        fr.append(c0 - g)
        xinj[0, f] = m1
        xinj[1, f] = p8
        xinj[2, f] = p8 - half_slope(p9 - p8, p8 - c7)
    fx = flux2(fl, fr, 0)
    for f in range(5):
        xinj[3, f] = fx[f]

    for z in range(12):
        s = [state[f, z + 2] + half * L[f, z] for f in range(5)]
        w = prims_of(s)
        for f in range(5):
            L[f, z] = s[f]
            W[f, z] = w[f]

    for z0 in range(0, 8, PAIR):
        w = load(W, z0, PAIR + 4)
        tz = z_term(w)
        c = [x[2:-2] for x in w]
        ty = y_term(c, load(E1, z0, PAIR), load(E2, z0, PAIR))

        def rows(j, f, z0=z0):
            return jnp.stack([xinj[j, f, pl.ds(z0 + d, 1), :] for d in range(PAIR)])

        row = iota(c[0].shape, 1)
        left, right, inj = [], [], []
        for f in range(5):
            x = c[f]
            nxt = jnp.where(row == 7, rows(1, f), rollto(x, -1, 1))
            prv = jnp.where(row == 0, rows(0, f), rollto(x, 1, 1))
            h = half_slope(nxt - x, x - prv)
            left.append(x + h)
            right.append(jnp.where(row == 7, rows(2, f), rollto(x - h, -1, 1)))
        fx = flux2(left, right, 0)
        for f in range(5):
            tx = fx[f] - jnp.where(row == 0, rows(3, f), rollto(fx[f], 1, 1))
            s = L[f, pl.ds(z0 + 2, PAIR)] + half * (tx + ty[f] + tz[f])
            adv[f, pl.ds(z0, PAIR)] = 0.5 * state[f, pl.ds(z0 + 4, PAIR)] + 0.5 * s


    hi, lo = split(adv[...].reshape(320, 128))
    y1 = mm(first[...], hi)
    y1 = y1[:56] + y1[56:] + mm(first[:56, :], lo)
    col = 0
    lhs_hi, lhs_lo = [], []
    for k, chunk in enumerate(CHUNKS):
        n = len(chunk)
        y2 = jnp.concatenate([y1[(col + i) * 8 : (col + i) * 8 + 8] for i in range(n)], axis=1)
        hi, lo = split(y2)
        rows = slice(col * 128, (col + n) * 128)
        v = mm(hi, second[0, rows, :]) + mm(lo, second[0, rows, :]) + mm(hi, second[1, rows, :])
        col += n
        vh = v.astype(BF16).astype(F32)
        vl = v - vh
        for f in range(5):
            lhs_hi.append(dest[k * 5 + f] * vh[f : f + 1, :])
            lhs_lo.append(dest[k * 5 + f] * vl[f : f + 1, :])
    lhs = jnp.concatenate([jnp.concatenate(lhs_hi, axis=1), jnp.concatenate(lhs_lo, axis=1)], axis=0)
    image = lax.dot_general(
        lhs.astype(BF16), spots, (((1,), (1,)), ((), ())), preferred_element_type=F32
    )
    image = image[:16] + image[16:]
    sa[...] = image
    ga[0] = image
    send(sa.at[pl.ds(0, 10)], ga.at[:, pl.ds(0, 10)], y_of, far_y, sem_a)

    for c in (all_y, all_w, all_q, all_h):
        c.wait_send()
    all_a.wait()

def place(adv, ga, pick, adv_out, snap_out, snap, sems):
    first = pltpu.make_async_copy(adv, adv_out, sems.at[0])
    first.start()
    hi, lo = split(ga[...].reshape(ga.shape[0] * 16, 128))
    snap[...] = mm(pick[...], hi) + mm(pick[...], lo)
    second = pltpu.make_async_copy(snap, snap_out, sems.at[1])
    second.start()
    first.wait()
    second.wait()


def shards(ngx, ngy, state, counts, aggregator):
    first, second, ranks, cmat = tables()
    vm = pltpu.VMEM
    dma = pltpu.SemaphoreType.DMA
    vmem = pl.BlockSpec(memory_space=pltpu.VMEM)
    adv, images, pick = pl.pallas_call(
        functools.partial(kernel, ngx, ngy),
        out_shape=(
            vm((5, 8, 8, 128), F32),
            vm((ngy, 16, 128), F32),
            vm((ngy * 5, ngy * 16), BF16),
        ),
        in_specs=[pl.BlockSpec(memory_space=pltpu.HBM)] * 7,
        out_specs=(vmem, vmem, vmem),
        scratch_shapes=[
            vm(state.shape, F32),
            vm(counts.shape, jnp.int32),
            vm((1, 1), jnp.int32),
            vm(first.shape, BF16),
            vm(second.shape, BF16),
            vm(ranks.shape, jnp.int32),
            vm(cmat.shape, F32),
            dma((9,)),
            vm((5, 16, 8, 128), F32),
            vm((5, 12, 8, 128), F32),
            vm((5, 12, 8, 128), F32),
            vm((5, 12, 8, 128), F32),
            vm((5, 12, 8, 128), F32),
            vm((5, 12, 8, 128), F32),
            vm((5, 12, 8, 128), F32),
            vm((5, 8, 8, 128), F32),
            vm((5, 8, 8, 128), F32),
            vm((2, 5, 6, 8, 128), F32),
            vm((2, 5, 6, 8, 128), F32),
            vm((5, 8, 128), F32),
            vm((6, 5, 8, 128), F32),
            vm((2, 5, 2, 8, 128), F32),
            vm((2, 1, 128), F32),
            vm((ngy, 1, 128), F32),
            vm((ngx, 1, 128), F32),
            vm((ngy, 128), F32),
            vm((16, 128), F32),
            vm((2, 5, 7, 8, 128), F32),
            vm((4, 5, 8, 128), F32),
            dma((2,)), dma((2,)), dma((2,)), dma((2,)), dma((2,)),
        ],
        compiler_params=pltpu.CompilerParams(collective_id=0, has_side_effects=True),
        name="step",
    )(state, counts, aggregator.reshape(1, 1), first, second, ranks, cmat)
    hbm = pl.BlockSpec(memory_space=pltpu.HBM)
    adv, snap = pl.pallas_call(
        place,
        out_shape=(jax.ShapeDtypeStruct(adv.shape, F32), jax.ShapeDtypeStruct((ngy * 5, 128), F32)),
        in_specs=[vmem] * 3,
        out_specs=(hbm, hbm),
        scratch_shapes=[vm((ngy * 5, 128), F32), dma((2,))],
        compiler_params=pltpu.CompilerParams(vmem_limit_bytes=1 << 20),
        name="place",
    )(adv, images, pick)
    return adv, snap.reshape(1, 1, ngy * 640)


def solution(mesh):
    ngx, ngy = mesh.shape["gx"], mesh.shape["gy"]
    placed = (P(None, None, "gx", "gy"), P(None, None, "gx", "gy"), P("gx"))
    return jax.shard_map(
        functools.partial(shards, ngx, ngy),
        mesh=mesh,
        in_specs=placed,
        out_specs=(P(None, None, "gx", "gy"), P("gx", "gy", None)),
        check_vma=False,
    )
```

```python
import functools
import math

import jax
import jax.numpy as jnp
import numpy as np
from jax import lax
from jax.experimental import pallas as pl
from jax.experimental.pallas import tpu as pltpu
from jax.sharding import PartitionSpec as P

MESH = pl.DeviceIdType.MESH
F32 = jnp.float32
BF16 = jnp.bfloat16
GAMMA = 1.4
COURANT = 0.1
PAIR = 2
CORNERS = [(0, -1), (0, 1), (1, -1), (-1, -1), (1, 1), (-1, 1)]
CHUNKS = [[((0, 0), 4), ((0, 1), 3), ((0, 3), 1)], [((0, 2), 2), ((1, 0), 3), ((1, 1), 1), ((2, 0), 1)]]
COMBOS = [c for chunk in CHUNKS for c, _ in chunk]


def cosine_np():
    k = np.arange(8)[:, None]
    n = np.arange(8)[None, :]
    w = np.where(k == 0, math.sqrt(0.125), 0.5)
    return np.cos(math.pi * (2 * n + 1) * k / 16.0) * w


def rank_of():
    flat = np.arange(512)
    keys = (flat // 64 + flat // 8 % 8 + flat % 8) * 512 + flat
    order = np.argsort(keys, kind="stable")
    rank = np.empty(512, np.int64)
    rank[order] = np.arange(512)
    return rank.reshape(8, 8, 8)


def tables():
    c = cosine_np()
    rank = rank_of()
    first = np.zeros((56, 320), np.float32)
    for i, (kz, kx) in enumerate(COMBOS):
        for f in range(5):
            first[i * 8 + f, f * 64 : f * 64 + 64] = np.outer(c[kz], c[kx]).reshape(64)
    second = np.zeros((len(COMBOS) * 128, 128), np.float32)
    ranks = np.full((2, 128), 1000, np.int32)
    row = 0
    for k, chunk in enumerate(CHUNKS):
        slot = 0
        for (kz, kx), n in chunk:
            for ky in range(n):
                for b in range(16):
                    second[row * 128 + b * 8 : row * 128 + b * 8 + 8, slot * 16 + b] = c[ky]
                ranks[k, slot * 16 : slot * 16 + 16] = rank[kz, kx, ky]
                slot += 1
            row += 1
    b = np.arange(16)[:, None]
    lane = np.arange(128)[None, :] % 16
    count = np.concatenate([(b < lane), (b == lane), np.ones((16, 128))], axis=1).astype(np.float32)
    first_hi = first.astype(BF16)
    first_lo = (first - first_hi.astype(np.float32)).astype(BF16)
    second_hi = second.astype(BF16)
    second_lo = (second - second_hi.astype(np.float32)).astype(BF16)
    return np.concatenate([first_hi, first_lo]), np.stack([second_hi, second_lo]), ranks, count


def half_slope(a, b):
    return 0.5 * jnp.maximum(jnp.minimum(a, jnp.maximum(b, 0.0)), jnp.minimum(b, 0.0))


def prims_of(cons):
    rho, mx, my, mz, en = cons
    inv = 1.0 / rho
    u, v, w = mx * inv, my * inv, mz * inv
    p = (GAMMA - 1.0) * (en - 0.5 * (mx * u + my * v + mz * w))
    return [rho, u, v, w, p]


def root(x):
    return x * lax.rsqrt(jnp.maximum(x, 1e-37))


def flux2(left, right, comp):
    a = None
    for q in (left, right):
        s = jnp.abs(q[1 + comp]) + root(GAMMA * q[4] / q[0])
        a = s if a is None else jnp.maximum(a, s)
    out = None
    for q, away in ((left, None), (right, a)):
        rho, p, vel = q[0], q[4], q[1:4]
        vn = vel[comp]
        shift = vn + a if away is None else vn - a
        mass = rho * shift
        kin = 0.5 * (vel[0] * vel[0] + vel[1] * vel[1] + vel[2] * vel[2])
        rows = [mass] + [mass * v for v in vel]
        rows[1 + comp] = rows[1 + comp] + p
        rows.append(mass * kin + p * (shift * (1.0 / (GAMMA - 1.0)) + vn))
        out = rows if out is None else [x + y for x, y in zip(out, rows)]
    return out


def split(x):
    hi = x.astype(BF16)
    return hi, (x - hi.astype(F32)).astype(BF16)


def mm(a, b):
    return jnp.dot(a, b, preferred_element_type=F32)


def rollto(x, shift, axis):
    n = x.shape[axis]
    shift %= n
    return pltpu.roll(x, shift, axis) if shift else x


def last(x):
    return x.ndim - 1


def iota(shape, dim):
    return lax.broadcasted_iota(jnp.int32, shape, dim)


def z_term(w):
    out_l, out_r = [], []
    for x in w:
        d = x[1:] - x[:-1]
        h = half_slope(d[1:], d[:-1])
        c = x[1:-1]
        out_l.append((c + h)[:-1])
        out_r.append((c - h)[1:])
    f = flux2(out_l, out_r, 2)
    return [x[1:] - x[:-1] for x in f]


def x_next(a, b):
    row = iota(a.shape, a.ndim - 2)
    return jnp.where(row == 7, rollto(b, -1, b.ndim - 2), rollto(a, -1, a.ndim - 2))


def x_prev(a, b):
    row = iota(a.shape, a.ndim - 2)
    return jnp.where(row == 0, rollto(b, 1, b.ndim - 2), rollto(a, 1, a.ndim - 2))


def x_terms(a, b):
    la, ra, lb, rb = [], [], [], []
    for x, y in zip(a, b):
        fx, fy = x_next(x, y) - x, x_next(y, x) - y
        hx, hy = half_slope(fx, x_prev(fx, fy)), half_slope(fy, x_prev(fy, fx))
        la.append(x + hx)
        lb.append(y + hy)
        wx, wy = x - hx, y - hy
        ra.append(x_next(wx, wy))
        rb.append(x_next(wy, wx))
    fa, fb = flux2(la, ra, 0), flux2(lb, rb, 0)
    ta = [x - x_prev(x, y) for x, y in zip(fa, fb)]
    tb = [y - x_prev(y, x) for x, y in zip(fa, fb)]
    return ta, tb


def y_term(w, e1, e2):
    lane = iota(w[0].shape, last(w[0]))
    left, right = [], []
    for x, e, g in zip(w, e1, e2):
        nxt = jnp.where(lane == 127, e, rollto(x, -1, last(x)))
        prv = jnp.where(lane == 0, e, rollto(x, 1, last(x)))
        h = half_slope(nxt - x, x - prv)
        left.append(x + h)
        right.append(jnp.where(lane == 127, g, rollto(x - h, -1, last(x))))
    f = flux2(left, right, 1)
    return [x - jnp.where(lane == 0, g, rollto(x, 1, last(x))) for x, g in zip(f, e2)]


def packed_y(w):
    left, right = [], []
    for x in w:
        d = rollto(x, -1, last(x)) - x
        h = half_slope(d, rollto(d, 1, last(d)))
        left.append(x + h)
        right.append(x - h)
    f = flux2(left, [rollto(x, -1, last(x)) for x in right], 1)
    return right, f


def packed_z(w):
    left, right = [], []
    for x in w:
        d = rollto(x, -8, last(x)) - x
        h = half_slope(d, rollto(d, 8, last(d)))
        left.append(x + h)
        right.append(x - h)
    f = flux2(left, [rollto(x, -8, last(x)) for x in right], 2)
    return [x - rollto(x, 8, last(x)) for x in f]


def edge_lanes(low, high):
    col = iota(low.shape, last(low)) % 8
    return jnp.where(col == 7, rollto(high, 3, last(high)), rollto(low, 5, last(low)))


def pack_columns(planes, zs):
    out = None
    for z in zs:
        r = rollto(planes(z), 8 * z + 4, 1)
        out = r if out is None else jnp.where(iota(r.shape, 1) // 8 == z, r, out)
    return out


def kernel(
    ngx, ngy, state_in, counts_in, agg_in, first_in, second_in, ranks_in, cmat_in,
    adv, ga, pick,
    state, counts, agg, first, second, ranks, cmat, sem_in,
    W, XH, L, Lx, Wx, E1, E2, E1x, E2x, sendx, recvx, qown, recvq, qx,
    maxsend, ry, rw, tot,
    sa, xedge, xinj,
    sem_h, sem_q, sem_y, sem_w, sem_a,
):
    loads = [
        pltpu.make_async_copy(src, dst, sem_in.at[i])
        for i, (src, dst) in enumerate(
            [(state_in.at[:, 4:12], state.at[:, 4:12]), (counts_in, counts), (cmat_in, cmat)]
            + [(state_in.at[:, 0:4], state.at[:, 0:4]), (state_in.at[:, 12:16], state.at[:, 12:16])]
            + [(agg_in, agg), (ranks_in, ranks), (first_in, first), (second_in, second)]
        )
    ]
    for c in loads:
        c.start()

    gx = lax.axis_index("gx")
    gy = lax.axis_index("gy")

    def at(dx, dy):
        x = lax.rem(gx + (dx % ngx), ngx) if dx else gx
        y = lax.rem(gy + (dy % ngy), ngy) if dy else gy
        return (x, y)

    y_peers = [at(0, k) for k in range(1, ngy)]
    w_peers = [at(k, 0) for k in range(1, ngx)]
    halo_peers = [at(-1, 0), at(1, 0)]
    q_peers = [at(-dx, -dy) for dx, dy in CORNERS]

    barrier = pltpu.get_barrier_semaphore()
    far_w = sorted(range(1, ngx), key=lambda k: abs(k - ngx // 2))
    far_y = sorted(range(1, ngy), key=lambda k: abs(k - ngy // 2))
    everyone = [y_peers[k - 1] for k in far_y] + [w_peers[k - 1] for k in far_w] + q_peers[2:]
    for peer in everyone:
        pl.semaphore_signal(barrier, inc=1, device_id=peer, device_id_type=MESH)

    for c in loads[:3]:
        c.wait()
    vmax = None
    for z in range(4, 12):
        w = prims_of([state[f, z] for f in range(5)])
        for f in range(5):
            W[f, z] = w[f]
        c = root(GAMMA * w[4] / w[0])
        s = jnp.maximum(jnp.maximum(jnp.abs(w[1]), jnp.abs(w[2])), jnp.abs(w[3])) + c
        vmax = s if vmax is None else jnp.maximum(vmax, s)
    top = jnp.max(jnp.max(vmax, axis=0, keepdims=True), axis=1, keepdims=True)

    cnt = jnp.zeros((8, 16), F32)
    row16 = iota((8, 16), 0)
    for f in range(5):
        cnt = jnp.where(row16 == f, counts[f, 0].astype(F32), cnt)
    cexp = jnp.dot(cnt, cmat[...], preferred_element_type=F32)
    total = jnp.sum(cexp[:, 256:384], axis=0, keepdims=True)
    lane1 = iota((1, 128), 1)
    maxsend[0] = jnp.where(lane1 < 64, top, total)
    ry[0] = maxsend[0]

    pl.semaphore_wait(barrier, len(everyone))

    def send(src, bufs, peers, order, sems):
        for k in order:
            pltpu.make_async_remote_copy(
                src_ref=src, dst_ref=bufs.at[k], send_sem=sems.at[0], recv_sem=sems.at[1],
                device_id=peers[k], device_id_type=MESH,
            ).start()

    def whole(ref, sems):
        return pltpu.make_async_remote_copy(
            src_ref=ref, dst_ref=ref, send_sem=sems.at[0], recv_sem=sems.at[1],
            device_id=y_peers[0], device_id_type=MESH,
        )

    y_of = dict(zip(range(1, ngy), y_peers))
    w_of = dict(zip(range(1, ngx), w_peers))
    all_y, all_w = whole(ry.at[pl.ds(1, ngy - 1)], sem_y), whole(rw.at[pl.ds(1, ngx - 1)], sem_w)
    all_q, all_h = whole(recvq, sem_q), whole(recvx, sem_h)
    all_a = whole(ga.at[pl.ds(1, ngy - 1), pl.ds(0, 10)], sem_a)
    send(maxsend.at[0], ry, y_of, far_y, sem_y)
    for c in loads[3:]:
        c.wait()
    row8 = iota((8, 128), 0)
    for f in range(5):
        for k in range(6):
            lo, hi = state[f, 2 + k], state[f, 8 + k]
            sendx[0, f, k] = jnp.where(row8 < 4, lo, rollto(hi, 4, 0))
            sendx[1, f, k] = jnp.where(row8 < 4, rollto(lo, 4, 0), hi)
        qown[f] = pack_columns(lambda z: state[f, z], range(16))
    send(qown, recvq, q_peers, range(6), sem_q)
    for i, peer in enumerate(halo_peers):
        pltpu.make_async_remote_copy(
            src_ref=sendx.at[i], dst_ref=recvx.at[i], send_sem=sem_h.at[0], recv_sem=sem_h.at[1],
            device_id=peer, device_id_type=MESH,
        ).start()
    for z in (*range(0, 4), *range(12, 16)):
        w = prims_of([state[f, z] for f in range(5)])
        for f in range(5):
            W[f, z] = w[f]

    def load(ref, start, n):
        return [ref[f, pl.ds(start, n)] for f in range(5)]

    def z_main(i, carry):
        z0 = i * PAIR
        t = z_term(load(W, z0, PAIR + 4))
        for f in range(5):
            L[f, pl.ds(z0, PAIR)] = t[f]
        return carry

    lax.fori_loop(0, 12 // PAIR, z_main, 0)

    all_y.wait_recv()
    best = ry[0]
    for k in range(ngy):
        if k:
            best = jnp.maximum(best, ry[k])
        tot[k : k + 1, :] = jnp.where(lane1 < 64, rollto(ry[k], 64, 1), ry[k])
    maxsend[1] = jnp.where(lane1 < 64, best, rollto(best, 64, 1))
    send(maxsend.at[1], rw, w_of, far_w, sem_w)

    all_q.wait_recv()
    all_h.wait_recv()
    for f in range(5):
        for k in range(6):
            a, b = recvx[0, f, k], recvx[1, f, k]
            XH[f, k] = jnp.where(row8 < 4, a, rollto(b, 4, 0))
            XH[f, k + 6] = jnp.where(row8 < 4, rollto(a, 4, 0), b)
    for z in range(12):
        w = prims_of([XH[f, z] for f in range(5)])
        for f in range(5):
            Wx[f, z] = w[f]
    colm = iota((8, 128), 1) % 8
    packed = []
    for f in range(5):
        q = qown[f]
        qh = pack_columns(lambda z: XH[f, z - 2], range(2, 14))
        lo = jnp.where(row8 < 4, recvq[2, f], recvq[3, f])
        hi = jnp.where(row8 < 4, recvq[4, f], recvq[5, f])
        packed.append(
            jnp.stack(
                [
                    jnp.where(colm < 4, recvq[0, f], q),
                    jnp.where(colm < 4, q, recvq[1, f]),
                    jnp.where(colm < 4, lo, qh),
                    jnp.where(colm < 4, qh, hi),
                ]
            )
        )
    pw = prims_of(packed)
    pr, pf = packed_y(pw)
    ta, _ = x_terms([x[:2] for x in pw], [x[2:] for x in pw])
    tz = packed_z([x[:2] for x in pw])
    for f in range(5):
        ty = pf[f] - rollto(pf[f], 1, 2)
        qx[0, f] = packed[f][:2]
        qx[1, f] = ta[f] + tz[f] + ty[:2]

    def inject(e1, e2, pw, pr, pf, low, high, planes, offset):
        for f in range(5):
            c1 = edge_lanes(pw[f][low], pw[f][high])
            c2 = edge_lanes(pf[f][low], pr[f][high])
            for z in planes:
                e1[f, z - offset] = rollto(c1, -(8 * z + 8), 1)
                e2[f, z - offset] = rollto(c2, -(8 * z + 8), 1)

    inject(E1, E2, pw, pr, pf, 0, 1, range(2, 14), 2)
    inject(E1x, E2x, pw, pr, pf, 2, 3, range(4, 12), 4)

    def xy_main(i, carry):
        z0 = i * PAIR
        a = load(W, z0 + 2, PAIR)
        ta, tb = x_terms(a, load(Wx, z0, PAIR))
        ty = y_term(a, load(E1, z0, PAIR), load(E2, z0, PAIR))
        for f in range(5):
            L[f, pl.ds(z0, PAIR)] = L[f, pl.ds(z0, PAIR)] + ta[f] + ty[f]
            Lx[f, pl.ds(z0, PAIR)] = tb[f]
        return carry

    lax.fori_loop(0, 12 // PAIR, xy_main, 0)

    def strip(i, carry):
        z0 = i * PAIR
        w = load(Wx, z0, PAIR + 4)
        tz = z_term(w)
        ty = y_term([x[2:-2] for x in w], load(E1x, z0, PAIR), load(E2x, z0, PAIR))
        for f in range(5):
            Lx[f, pl.ds(z0 + 2, PAIR)] = Lx[f, pl.ds(z0 + 2, PAIR)] + tz[f] + ty[f]
        return carry

    lax.fori_loop(0, 8 // PAIR, strip, 0)
    for f in range(5):
        for j, r in enumerate((6, 7, 0, 1)):
            for z in range(8):
                xedge[0, f, j, z : z + 1, :] = XH[f, z + 2, r : r + 1, :]
                xedge[1, f, j, z : z + 1, :] = Lx[f, z + 2, r : r + 1, :]
        for j, r in enumerate((0, 1, 7)):
            for z in range(8):
                xedge[0, f, j + 4, z : z + 1, :] = state[f, z + 4, r : r + 1, :]
                xedge[1, f, j + 4, z : z + 1, :] = L[f, z + 2, r : r + 1, :]

    leader = agg[...]
    me_rank = (gy - leader + ngy) & (ngy - 1)
    nlane = ngy * 16
    slot_col = iota((ngy, nlane), 0)
    slot_row = iota((ngy, nlane), 1) // 16

    def turn(slot):
        return (gy - slot - leader + 2 * ngy) & (ngy - 1)

    totals = tot[...]
    wide = jnp.broadcast_to(totals[:, :1], (ngy, nlane))
    before = jnp.where(turn(slot_col) < turn(slot_row), wide, 0.0)
    starts = jnp.sum(before, axis=0, keepdims=True).astype(jnp.int32)
    mine = jnp.sum(
        jnp.where(turn(iota((ngy, 128), 0)) < me_rank, totals, 0.0), axis=0, keepdims=True
    ).astype(jnp.int32)
    field_total = cexp[:, 256:384]
    upto = cexp[:, :128]
    for f in range(4):
        upto = upto + jnp.where(row8 > f, field_total[f : f + 1, :], 0.0)
    own_count = cexp[:, 128:256].astype(jnp.int32)
    base = upto.astype(jnp.int32) + (mine & 127)
    dest, spots = [], []
    for k in range(2):
        rank = ranks[k : k + 1, :]
        pos = base + rank
        keep = rank < own_count
        row_to = jnp.where(keep, pos >> 7, -1)
        lane_to = pos & 127
        for f in range(5):
            dest.append(row_to[f : f + 1, :])
            spots.append((iota((128, 128), 0) == lane_to[f : f + 1, :]).astype(F32).astype(BF16))
    spots = jnp.concatenate(spots, axis=1)
    dest = [(iota((16, 128), 0) == d).astype(F32) for d in dest]

    nrow = ngy * 5
    q = iota((nrow, nlane), 0)
    lead = me_rank == 0
    in_row = q - (starts >> 7)
    pick[...] = jnp.where((in_row == iota((nrow, nlane), 1) % 16) & lead, 1.0, 0.0).astype(BF16)
    ga[:, 10:16] = jnp.zeros((ngy, 6, 128), F32)

    all_w.wait_recv()
    best = maxsend[1]
    for k in range(1, ngx):
        best = jnp.maximum(best, rw[k])
    ratio = COURANT / best
    half = -0.5 * ratio

    p1 = prims_of([qx[0, f] + half * qx[1, f] for f in range(5)])
    pr, pf = packed_y(p1)
    inject(E1, E2, p1, pr, pf, 0, 1, range(4, 12), 4)
    we = prims_of([xedge[0, f] + half * xedge[1, f] for f in range(5)])
    fl, fr = [], []
    for f in range(5):
        m2, m1, p8, p9, c0, c1, c7 = [we[f][j] for j in range(7)]
        h = half_slope(c0 - m1, m1 - m2)
        g = half_slope(c1 - c0, c0 - m1)
        fl.append(m1 + h)
        fr.append(c0 - g)
        xinj[0, f] = m1
        xinj[1, f] = p8
        xinj[2, f] = p8 - half_slope(p9 - p8, p8 - c7)
    fx = flux2(fl, fr, 0)
    for f in range(5):
        xinj[3, f] = fx[f]

    for z in range(12):
        s = [state[f, z + 2] + half * L[f, z] for f in range(5)]
        w = prims_of(s)
        for f in range(5):
            L[f, z] = s[f]
            W[f, z] = w[f]

    for z0 in range(0, 8, 4):
        w = load(W, z0, 4 + 4)
        tz = z_term(w)
        c = [x[2:-2] for x in w]
        ty = y_term(c, load(E1, z0, 4), load(E2, z0, 4))

        def rows(j, f, z0=z0):
            return jnp.stack([xinj[j, f, pl.ds(z0 + d, 1), :] for d in range(4)])

        row = iota(c[0].shape, 1)
        left, right, inj = [], [], []
        for f in range(5):
            x = c[f]
            nxt = jnp.where(row == 7, rows(1, f), rollto(x, -1, 1))
            prv = jnp.where(row == 0, rows(0, f), rollto(x, 1, 1))
            h = half_slope(nxt - x, x - prv)
            left.append(x + h)
            right.append(jnp.where(row == 7, rows(2, f), rollto(x - h, -1, 1)))
        fx = flux2(left, right, 0)
        for f in range(5):
            tx = fx[f] - jnp.where(row == 0, rows(3, f), rollto(fx[f], 1, 1))
            s = L[f, pl.ds(z0 + 2, 4)] + half * (tx + ty[f] + tz[f])
            adv[f, pl.ds(z0, 4)] = 0.5 * state[f, pl.ds(z0 + 4, 4)] + 0.5 * s


    hi, lo = split(adv[...].reshape(320, 128))
    y1 = mm(first[...], hi)
    y1 = y1[:56] + y1[56:] + mm(first[:56, :], lo)
    col = 0
    lhs_hi, lhs_lo = [], []
    for k, chunk in enumerate(CHUNKS):
        n = len(chunk)
        y2 = jnp.concatenate([y1[(col + i) * 8 : (col + i) * 8 + 8] for i in range(n)], axis=1)
        hi, lo = split(y2)
        rows = slice(col * 128, (col + n) * 128)
        v = mm(hi, second[0, rows, :]) + mm(lo, second[0, rows, :]) + mm(hi, second[1, rows, :])
        col += n
        vh = v.astype(BF16).astype(F32)
        vl = v - vh
        for f in range(5):
            lhs_hi.append(dest[k * 5 + f] * vh[f : f + 1, :])
            lhs_lo.append(dest[k * 5 + f] * vl[f : f + 1, :])
    lhs = jnp.concatenate([jnp.concatenate(lhs_hi, axis=1), jnp.concatenate(lhs_lo, axis=1)], axis=0)
    image = lax.dot_general(
        lhs.astype(BF16), spots, (((1,), (1,)), ((), ())), preferred_element_type=F32
    )
    image = image[:16] + image[16:]
    sa[...] = image
    ga[0] = image
    send(sa.at[pl.ds(0, 10)], ga.at[:, pl.ds(0, 10)], y_of, far_y, sem_a)

    for c in (all_y, all_w, all_q, all_h):
        c.wait_send()
    all_a.wait()

def place(adv, ga, pick, adv_out, snap_out, snap, sems):
    first = pltpu.make_async_copy(adv, adv_out, sems.at[0])
    first.start()
    hi, lo = split(ga[...].reshape(ga.shape[0] * 16, 128))
    snap[...] = mm(pick[...], hi) + mm(pick[...], lo)
    second = pltpu.make_async_copy(snap, snap_out, sems.at[1])
    second.start()
    first.wait()
    second.wait()


def shards(ngx, ngy, state, counts, aggregator):
    first, second, ranks, cmat = tables()
    vm = pltpu.VMEM
    dma = pltpu.SemaphoreType.DMA
    vmem = pl.BlockSpec(memory_space=pltpu.VMEM)
    adv, images, pick = pl.pallas_call(
        functools.partial(kernel, ngx, ngy),
        out_shape=(
            vm((5, 8, 8, 128), F32),
            vm((ngy, 16, 128), F32),
            vm((ngy * 5, ngy * 16), BF16),
        ),
        in_specs=[pl.BlockSpec(memory_space=pltpu.HBM)] * 7,
        out_specs=(vmem, vmem, vmem),
        scratch_shapes=[
            vm(state.shape, F32),
            vm(counts.shape, jnp.int32),
            vm((1, 1), jnp.int32),
            vm(first.shape, BF16),
            vm(second.shape, BF16),
            vm(ranks.shape, jnp.int32),
            vm(cmat.shape, F32),
            dma((9,)),
            vm((5, 16, 8, 128), F32),
            vm((5, 12, 8, 128), F32),
            vm((5, 12, 8, 128), F32),
            vm((5, 12, 8, 128), F32),
            vm((5, 12, 8, 128), F32),
            vm((5, 12, 8, 128), F32),
            vm((5, 12, 8, 128), F32),
            vm((5, 8, 8, 128), F32),
            vm((5, 8, 8, 128), F32),
            vm((2, 5, 6, 8, 128), F32),
            vm((2, 5, 6, 8, 128), F32),
            vm((5, 8, 128), F32),
            vm((6, 5, 8, 128), F32),
            vm((2, 5, 2, 8, 128), F32),
            vm((2, 1, 128), F32),
            vm((ngy, 1, 128), F32),
            vm((ngx, 1, 128), F32),
            vm((ngy, 128), F32),
            vm((16, 128), F32),
            vm((2, 5, 7, 8, 128), F32),
            vm((4, 5, 8, 128), F32),
            dma((2,)), dma((2,)), dma((2,)), dma((2,)), dma((2,)),
        ],
        compiler_params=pltpu.CompilerParams(collective_id=0, has_side_effects=True),
        name="step",
    )(state, counts, aggregator.reshape(1, 1), first, second, ranks, cmat)
    hbm = pl.BlockSpec(memory_space=pltpu.HBM)
    adv, snap = pl.pallas_call(
        place,
        out_shape=(jax.ShapeDtypeStruct(adv.shape, F32), jax.ShapeDtypeStruct((ngy * 5, 128), F32)),
        in_specs=[vmem] * 3,
        out_specs=(hbm, hbm),
        scratch_shapes=[vm((ngy * 5, 128), F32), dma((2,))],
        compiler_params=pltpu.CompilerParams(vmem_limit_bytes=1 << 20),
        name="place",
    )(adv, images, pick)
    return adv, snap.reshape(1, 1, ngy * 640)


def solution(mesh):
    ngx, ngy = mesh.shape["gx"], mesh.shape["gy"]
    placed = (P(None, None, "gx", "gy"), P(None, None, "gx", "gy"), P("gx"))
    return jax.shard_map(
        functools.partial(shards, ngx, ngy),
        mesh=mesh,
        in_specs=placed,
        out_specs=(P(None, None, "gx", "gy"), P("gx", "gy", None)),
        check_vma=False,
    )
```

```python
import functools
import math

import jax
import jax.numpy as jnp
import numpy as np
from jax import lax
from jax.experimental import pallas as pl
from jax.experimental.pallas import tpu as pltpu
from jax.sharding import PartitionSpec as P

MESH = pl.DeviceIdType.MESH
F32 = jnp.float32
BF16 = jnp.bfloat16
GAMMA = 1.4
COURANT = 0.1
PAIR = 2
CORNERS = [(0, -1), (0, 1), (1, -1), (-1, -1), (1, 1), (-1, 1)]
CHUNKS = [[((0, 0), 4), ((0, 1), 3), ((0, 3), 1)], [((0, 2), 2), ((1, 0), 3), ((1, 1), 1), ((2, 0), 1)]]
COMBOS = [c for chunk in CHUNKS for c, _ in chunk]


def cosine_np():
    k = np.arange(8)[:, None]
    n = np.arange(8)[None, :]
    w = np.where(k == 0, math.sqrt(0.125), 0.5)
    return np.cos(math.pi * (2 * n + 1) * k / 16.0) * w


def rank_of():
    flat = np.arange(512)
    keys = (flat // 64 + flat // 8 % 8 + flat % 8) * 512 + flat
    order = np.argsort(keys, kind="stable")
    rank = np.empty(512, np.int64)
    rank[order] = np.arange(512)
    return rank.reshape(8, 8, 8)


def tables():
    c = cosine_np()
    rank = rank_of()
    first = np.zeros((56, 320), np.float32)
    for i, (kz, kx) in enumerate(COMBOS):
        for f in range(5):
            first[i * 8 + f, f * 64 : f * 64 + 64] = np.outer(c[kz], c[kx]).reshape(64)
    second = np.zeros((len(COMBOS) * 128, 128), np.float32)
    ranks = np.full((2, 128), 1000, np.int32)
    row = 0
    for k, chunk in enumerate(CHUNKS):
        slot = 0
        for (kz, kx), n in chunk:
            for ky in range(n):
                for b in range(16):
                    second[row * 128 + b * 8 : row * 128 + b * 8 + 8, slot * 16 + b] = c[ky]
                ranks[k, slot * 16 : slot * 16 + 16] = rank[kz, kx, ky]
                slot += 1
            row += 1
    b = np.arange(16)[:, None]
    lane = np.arange(128)[None, :] % 16
    count = np.concatenate([(b < lane), (b == lane), np.ones((16, 128))], axis=1).astype(np.float32)
    first_hi = first.astype(BF16)
    first_lo = (first - first_hi.astype(np.float32)).astype(BF16)
    second_hi = second.astype(BF16)
    second_lo = (second - second_hi.astype(np.float32)).astype(BF16)
    return np.concatenate([first_hi, first_lo]), np.stack([second_hi, second_lo]), ranks, count


def half_slope(a, b):
    return 0.5 * jnp.maximum(jnp.minimum(a, jnp.maximum(b, 0.0)), jnp.minimum(b, 0.0))


def prims_of(cons):
    rho, mx, my, mz, en = cons
    inv = 1.0 / rho
    u, v, w = mx * inv, my * inv, mz * inv
    p = (GAMMA - 1.0) * (en - 0.5 * (mx * u + my * v + mz * w))
    return [rho, u, v, w, p]


def root(x):
    return x * lax.rsqrt(jnp.maximum(x, 1e-37))


def flux2(left, right, comp):
    a = None
    for q in (left, right):
        s = jnp.abs(q[1 + comp]) + root(GAMMA * q[4] / q[0])
        a = s if a is None else jnp.maximum(a, s)
    out = None
    for q, away in ((left, None), (right, a)):
        rho, p, vel = q[0], q[4], q[1:4]
        vn = vel[comp]
        shift = vn + a if away is None else vn - a
        mass = rho * shift
        kin = 0.5 * (vel[0] * vel[0] + vel[1] * vel[1] + vel[2] * vel[2])
        rows = [mass] + [mass * v for v in vel]
        rows[1 + comp] = rows[1 + comp] + p
        rows.append(mass * kin + p * (shift * (1.0 / (GAMMA - 1.0)) + vn))
        out = rows if out is None else [x + y for x, y in zip(out, rows)]
    return out


def split(x):
    hi = x.astype(BF16)
    return hi, (x - hi.astype(F32)).astype(BF16)


def mm(a, b):
    return jnp.dot(a, b, preferred_element_type=F32)


def rollto(x, shift, axis):
    n = x.shape[axis]
    shift %= n
    return pltpu.roll(x, shift, axis) if shift else x


def last(x):
    return x.ndim - 1


def iota(shape, dim):
    return lax.broadcasted_iota(jnp.int32, shape, dim)


def z_term(w):
    out_l, out_r = [], []
    for x in w:
        d = x[1:] - x[:-1]
        h = half_slope(d[1:], d[:-1])
        c = x[1:-1]
        out_l.append((c + h)[:-1])
        out_r.append((c - h)[1:])
    f = flux2(out_l, out_r, 2)
    return [x[1:] - x[:-1] for x in f]


def x_next(a, b):
    row = iota(a.shape, a.ndim - 2)
    return jnp.where(row == 7, rollto(b, -1, b.ndim - 2), rollto(a, -1, a.ndim - 2))


def x_prev(a, b):
    row = iota(a.shape, a.ndim - 2)
    return jnp.where(row == 0, rollto(b, 1, b.ndim - 2), rollto(a, 1, a.ndim - 2))


def x_terms(a, b):
    la, ra, lb, rb = [], [], [], []
    for x, y in zip(a, b):
        fx, fy = x_next(x, y) - x, x_next(y, x) - y
        hx, hy = half_slope(fx, x_prev(fx, fy)), half_slope(fy, x_prev(fy, fx))
        la.append(x + hx)
        lb.append(y + hy)
        wx, wy = x - hx, y - hy
        ra.append(x_next(wx, wy))
        rb.append(x_next(wy, wx))
    fa, fb = flux2(la, ra, 0), flux2(lb, rb, 0)
    ta = [x - x_prev(x, y) for x, y in zip(fa, fb)]
    tb = [y - x_prev(y, x) for x, y in zip(fa, fb)]
    return ta, tb


def y_term(w, e1, e2):
    lane = iota(w[0].shape, last(w[0]))
    left, right = [], []
    for x, e, g in zip(w, e1, e2):
        nxt = jnp.where(lane == 127, e, rollto(x, -1, last(x)))
        prv = jnp.where(lane == 0, e, rollto(x, 1, last(x)))
        h = half_slope(nxt - x, x - prv)
        left.append(x + h)
        right.append(jnp.where(lane == 127, g, rollto(x - h, -1, last(x))))
    f = flux2(left, right, 1)
    return [x - jnp.where(lane == 0, g, rollto(x, 1, last(x))) for x, g in zip(f, e2)]


def packed_y(w):
    left, right = [], []
    for x in w:
        d = rollto(x, -1, last(x)) - x
        h = half_slope(d, rollto(d, 1, last(d)))
        left.append(x + h)
        right.append(x - h)
    f = flux2(left, [rollto(x, -1, last(x)) for x in right], 1)
    return right, f


def packed_z(w):
    left, right = [], []
    for x in w:
        d = rollto(x, -8, last(x)) - x
        h = half_slope(d, rollto(d, 8, last(d)))
        left.append(x + h)
        right.append(x - h)
    f = flux2(left, [rollto(x, -8, last(x)) for x in right], 2)
    return [x - rollto(x, 8, last(x)) for x in f]


def edge_lanes(low, high):
    col = iota(low.shape, last(low)) % 8
    return jnp.where(col == 7, rollto(high, 3, last(high)), rollto(low, 5, last(low)))


def pack_columns(planes, zs):
    out = None
    for z in zs:
        r = rollto(planes(z), 8 * z + 4, 1)
        out = r if out is None else jnp.where(iota(r.shape, 1) // 8 == z, r, out)
    return out


def kernel(
    ngx, ngy, state_in, counts_in, agg_in, first_in, second_in, ranks_in, cmat_in,
    adv, ga, pick,
    state, counts, agg, first, second, ranks, cmat, sem_in,
    W, XH, L, Lx, Wx, E1, E2, E1x, E2x, sendx, recvx, qown, recvq, qx,
    maxsend, ry, rw, tot,
    sa, xedge, xinj,
    sem_h, sem_q, sem_y, sem_w, sem_a,
):
    loads = [
        pltpu.make_async_copy(src, dst, sem_in.at[i])
        for i, (src, dst) in enumerate(
            [(state_in.at[:, 4:12], state.at[:, 4:12]), (counts_in, counts), (cmat_in, cmat)]
            + [(state_in.at[:, 0:4], state.at[:, 0:4]), (state_in.at[:, 12:16], state.at[:, 12:16])]
            + [(agg_in, agg), (ranks_in, ranks), (first_in, first), (second_in, second)]
        )
    ]
    for c in loads:
        c.start()

    gx = lax.axis_index("gx")
    gy = lax.axis_index("gy")

    def at(dx, dy):
        x = lax.rem(gx + (dx % ngx), ngx) if dx else gx
        y = lax.rem(gy + (dy % ngy), ngy) if dy else gy
        return (x, y)

    y_peers = [at(0, k) for k in range(1, ngy)]
    w_peers = [at(k, 0) for k in range(1, ngx)]
    halo_peers = [at(-1, 0), at(1, 0)]
    q_peers = [at(-dx, -dy) for dx, dy in CORNERS]

    barrier = pltpu.get_barrier_semaphore()
    far_w = sorted(range(1, ngx), key=lambda k: abs(k - ngx // 2))
    far_y = sorted(range(1, ngy), key=lambda k: abs(k - ngy // 2))
    everyone = [y_peers[k - 1] for k in far_y] + [w_peers[k - 1] for k in far_w] + q_peers[2:]
    for peer in everyone:
        pl.semaphore_signal(barrier, inc=1, device_id=peer, device_id_type=MESH)

    for c in loads[:3]:
        c.wait()
    vmax = None
    for z in range(4, 12):
        w = prims_of([state[f, z] for f in range(5)])
        for f in range(5):
            W[f, z] = w[f]
        c = root(GAMMA * w[4] / w[0])
        s = jnp.maximum(jnp.maximum(jnp.abs(w[1]), jnp.abs(w[2])), jnp.abs(w[3])) + c
        vmax = s if vmax is None else jnp.maximum(vmax, s)
    top = jnp.max(jnp.max(vmax, axis=0, keepdims=True), axis=1, keepdims=True)

    cnt = jnp.zeros((8, 16), F32)
    row16 = iota((8, 16), 0)
    for f in range(5):
        cnt = jnp.where(row16 == f, counts[f, 0].astype(F32), cnt)
    cexp = jnp.dot(cnt, cmat[...], preferred_element_type=F32)
    total = jnp.sum(cexp[:, 256:384], axis=0, keepdims=True)
    lane1 = iota((1, 128), 1)
    maxsend[0] = jnp.where(lane1 < 64, top, total)
    ry[0] = maxsend[0]

    pl.semaphore_wait(barrier, len(everyone))

    def send(src, bufs, peers, order, sems):
        for k in order:
            pltpu.make_async_remote_copy(
                src_ref=src, dst_ref=bufs.at[k], send_sem=sems.at[0], recv_sem=sems.at[1],
                device_id=peers[k], device_id_type=MESH,
            ).start()

    def whole(ref, sems):
        return pltpu.make_async_remote_copy(
            src_ref=ref, dst_ref=ref, send_sem=sems.at[0], recv_sem=sems.at[1],
            device_id=y_peers[0], device_id_type=MESH,
        )

    y_of = dict(zip(range(1, ngy), y_peers))
    w_of = dict(zip(range(1, ngx), w_peers))
    all_y, all_w = whole(ry.at[pl.ds(1, ngy - 1)], sem_y), whole(rw.at[pl.ds(1, ngx - 1)], sem_w)
    all_q, all_h = whole(recvq, sem_q), whole(recvx, sem_h)
    all_a = whole(ga.at[pl.ds(1, ngy - 1), pl.ds(0, 10)], sem_a)
    send(maxsend.at[0], ry, y_of, far_y, sem_y)
    for c in loads[3:]:
        c.wait()
    row8 = iota((8, 128), 0)
    for f in range(5):
        for k in range(6):
            lo, hi = state[f, 2 + k], state[f, 8 + k]
            sendx[0, f, k] = jnp.where(row8 < 4, lo, rollto(hi, 4, 0))
            sendx[1, f, k] = jnp.where(row8 < 4, rollto(lo, 4, 0), hi)
        qown[f] = pack_columns(lambda z: state[f, z], range(16))
    send(qown, recvq, q_peers, range(6), sem_q)
    for i, peer in enumerate(halo_peers):
        pltpu.make_async_remote_copy(
            src_ref=sendx.at[i], dst_ref=recvx.at[i], send_sem=sem_h.at[0], recv_sem=sem_h.at[1],
            device_id=peer, device_id_type=MESH,
        ).start()
    for z in (*range(0, 4), *range(12, 16)):
        w = prims_of([state[f, z] for f in range(5)])
        for f in range(5):
            W[f, z] = w[f]

    def load(ref, start, n):
        return [ref[f, pl.ds(start, n)] for f in range(5)]

    def z_main(i, carry):
        z0 = i * PAIR
        t = z_term(load(W, z0, PAIR + 4))
        for f in range(5):
            L[f, pl.ds(z0, PAIR)] = t[f]
        return carry

    lax.fori_loop(0, 12 // PAIR, z_main, 0)

    all_y.wait_recv()
    best = ry[0]
    for k in range(ngy):
        if k:
            best = jnp.maximum(best, ry[k])
        tot[k : k + 1, :] = jnp.where(lane1 < 64, rollto(ry[k], 64, 1), ry[k])
    maxsend[1] = jnp.where(lane1 < 64, best, rollto(best, 64, 1))
    send(maxsend.at[1], rw, w_of, far_w, sem_w)

    leader = agg[...]
    me_rank = (gy - leader + ngy) & (ngy - 1)
    nlane = ngy * 16
    slot_col = iota((ngy, nlane), 0)
    slot_row = iota((ngy, nlane), 1) // 16

    def turn(slot):
        return (gy - slot - leader + 2 * ngy) & (ngy - 1)

    totals = tot[...]
    wide = jnp.broadcast_to(totals[:, :1], (ngy, nlane))
    before = jnp.where(turn(slot_col) < turn(slot_row), wide, 0.0)
    starts = jnp.sum(before, axis=0, keepdims=True).astype(jnp.int32)
    mine = jnp.sum(
        jnp.where(turn(iota((ngy, 128), 0)) < me_rank, totals, 0.0), axis=0, keepdims=True
    ).astype(jnp.int32)
    field_total = cexp[:, 256:384]
    upto = cexp[:, :128]
    for f in range(4):
        upto = upto + jnp.where(row8 > f, field_total[f : f + 1, :], 0.0)
    own_count = cexp[:, 128:256].astype(jnp.int32)
    base = upto.astype(jnp.int32) + (mine & 127)
    dest, spots = [], []
    for k in range(2):
        rank = ranks[k : k + 1, :]
        pos = base + rank
        keep = rank < own_count
        row_to = jnp.where(keep, pos >> 7, -1)
        lane_to = pos & 127
        for f in range(5):
            dest.append(row_to[f : f + 1, :])
            spots.append((iota((128, 128), 0) == lane_to[f : f + 1, :]).astype(F32).astype(BF16))
    spots = jnp.concatenate(spots, axis=1)
    dest = [(iota((16, 128), 0) == d).astype(F32) for d in dest]

    nrow = ngy * 5
    q = iota((nrow, nlane), 0)
    lead = me_rank == 0
    in_row = q - (starts >> 7)
    pick[...] = jnp.where((in_row == iota((nrow, nlane), 1) % 16) & lead, 1.0, 0.0).astype(BF16)
    ga[:, 10:16] = jnp.zeros((ngy, 6, 128), F32)

    all_q.wait_recv()
    all_h.wait_recv()
    for f in range(5):
        for k in range(6):
            a, b = recvx[0, f, k], recvx[1, f, k]
            XH[f, k] = jnp.where(row8 < 4, a, rollto(b, 4, 0))
            XH[f, k + 6] = jnp.where(row8 < 4, rollto(a, 4, 0), b)
    for z in range(12):
        w = prims_of([XH[f, z] for f in range(5)])
        for f in range(5):
            Wx[f, z] = w[f]
    colm = iota((8, 128), 1) % 8
    packed = []
    for f in range(5):
        q = qown[f]
        qh = pack_columns(lambda z: XH[f, z - 2], range(2, 14))
        lo = jnp.where(row8 < 4, recvq[2, f], recvq[3, f])
        hi = jnp.where(row8 < 4, recvq[4, f], recvq[5, f])
        packed.append(
            jnp.stack(
                [
                    jnp.where(colm < 4, recvq[0, f], q),
                    jnp.where(colm < 4, q, recvq[1, f]),
                    jnp.where(colm < 4, lo, qh),
                    jnp.where(colm < 4, qh, hi),
                ]
            )
        )
    pw = prims_of(packed)
    pr, pf = packed_y(pw)
    ta, _ = x_terms([x[:2] for x in pw], [x[2:] for x in pw])
    tz = packed_z([x[:2] for x in pw])
    for f in range(5):
        ty = pf[f] - rollto(pf[f], 1, 2)
        qx[0, f] = packed[f][:2]
        qx[1, f] = ta[f] + tz[f] + ty[:2]

    def inject(e1, e2, pw, pr, pf, low, high, planes, offset):
        for f in range(5):
            c1 = edge_lanes(pw[f][low], pw[f][high])
            c2 = edge_lanes(pf[f][low], pr[f][high])
            for z in planes:
                e1[f, z - offset] = rollto(c1, -(8 * z + 8), 1)
                e2[f, z - offset] = rollto(c2, -(8 * z + 8), 1)

    inject(E1, E2, pw, pr, pf, 0, 1, range(2, 14), 2)
    inject(E1x, E2x, pw, pr, pf, 2, 3, range(4, 12), 4)

    def xy_main(i, carry):
        z0 = i * PAIR
        a = load(W, z0 + 2, PAIR)
        ta, tb = x_terms(a, load(Wx, z0, PAIR))
        ty = y_term(a, load(E1, z0, PAIR), load(E2, z0, PAIR))
        for f in range(5):
            L[f, pl.ds(z0, PAIR)] = L[f, pl.ds(z0, PAIR)] + ta[f] + ty[f]
            Lx[f, pl.ds(z0, PAIR)] = tb[f]
        return carry

    lax.fori_loop(0, 12 // PAIR, xy_main, 0)

    def strip(i, carry):
        z0 = i * PAIR
        w = load(Wx, z0, PAIR + 4)
        tz = z_term(w)
        ty = y_term([x[2:-2] for x in w], load(E1x, z0, PAIR), load(E2x, z0, PAIR))
        for f in range(5):
            Lx[f, pl.ds(z0 + 2, PAIR)] = Lx[f, pl.ds(z0 + 2, PAIR)] + tz[f] + ty[f]
        return carry

    lax.fori_loop(0, 8 // PAIR, strip, 0)
    for f in range(5):
        for j, r in enumerate((6, 7, 0, 1)):
            for z in range(8):
                xedge[0, f, j, z : z + 1, :] = XH[f, z + 2, r : r + 1, :]
                xedge[1, f, j, z : z + 1, :] = Lx[f, z + 2, r : r + 1, :]
        for j, r in enumerate((0, 1, 7)):
            for z in range(8):
                xedge[0, f, j + 4, z : z + 1, :] = state[f, z + 4, r : r + 1, :]
                xedge[1, f, j + 4, z : z + 1, :] = L[f, z + 2, r : r + 1, :]

    all_w.wait_recv()
    best = maxsend[1]
    for k in range(1, ngx):
        best = jnp.maximum(best, rw[k])
    ratio = COURANT / best
    half = -0.5 * ratio

    p1 = prims_of([qx[0, f] + half * qx[1, f] for f in range(5)])
    pr, pf = packed_y(p1)
    inject(E1, E2, p1, pr, pf, 0, 1, range(4, 12), 4)
    we = prims_of([xedge[0, f] + half * xedge[1, f] for f in range(5)])
    fl, fr = [], []
    for f in range(5):
        m2, m1, p8, p9, c0, c1, c7 = [we[f][j] for j in range(7)]
        h = half_slope(c0 - m1, m1 - m2)
        g = half_slope(c1 - c0, c0 - m1)
        fl.append(m1 + h)
        fr.append(c0 - g)
        xinj[0, f] = m1
        xinj[1, f] = p8
        xinj[2, f] = p8 - half_slope(p9 - p8, p8 - c7)
    fx = flux2(fl, fr, 0)
    for f in range(5):
        xinj[3, f] = fx[f]

    for z in range(12):
        s = [state[f, z + 2] + half * L[f, z] for f in range(5)]
        w = prims_of(s)
        for f in range(5):
            L[f, z] = s[f]
            W[f, z] = w[f]

    for z0 in range(0, 8, 4):
        w = load(W, z0, 4 + 4)
        tz = z_term(w)
        c = [x[2:-2] for x in w]
        ty = y_term(c, load(E1, z0, 4), load(E2, z0, 4))

        def rows(j, f, z0=z0):
            return jnp.stack([xinj[j, f, pl.ds(z0 + d, 1), :] for d in range(4)])

        row = iota(c[0].shape, 1)
        left, right, inj = [], [], []
        for f in range(5):
            x = c[f]
            nxt = jnp.where(row == 7, rows(1, f), rollto(x, -1, 1))
            prv = jnp.where(row == 0, rows(0, f), rollto(x, 1, 1))
            h = half_slope(nxt - x, x - prv)
            left.append(x + h)
            right.append(jnp.where(row == 7, rows(2, f), rollto(x - h, -1, 1)))
        fx = flux2(left, right, 0)
        for f in range(5):
            tx = fx[f] - jnp.where(row == 0, rows(3, f), rollto(fx[f], 1, 1))
            s = L[f, pl.ds(z0 + 2, 4)] + half * (tx + ty[f] + tz[f])
            adv[f, pl.ds(z0, 4)] = 0.5 * state[f, pl.ds(z0 + 4, 4)] + 0.5 * s


    hi, lo = split(adv[...].reshape(320, 128))
    y1 = mm(first[...], hi)
    y1 = y1[:56] + y1[56:] + mm(first[:56, :], lo)
    col = 0
    lhs_hi, lhs_lo = [], []
    for k, chunk in enumerate(CHUNKS):
        n = len(chunk)
        y2 = jnp.concatenate([y1[(col + i) * 8 : (col + i) * 8 + 8] for i in range(n)], axis=1)
        hi, lo = split(y2)
        rows = slice(col * 128, (col + n) * 128)
        v = mm(hi, second[0, rows, :]) + mm(lo, second[0, rows, :]) + mm(hi, second[1, rows, :])
        col += n
        vh = v.astype(BF16).astype(F32)
        vl = v - vh
        for f in range(5):
            lhs_hi.append(dest[k * 5 + f] * vh[f : f + 1, :])
            lhs_lo.append(dest[k * 5 + f] * vl[f : f + 1, :])
    lhs = jnp.concatenate([jnp.concatenate(lhs_hi, axis=1), jnp.concatenate(lhs_lo, axis=1)], axis=0)
    image = lax.dot_general(
        lhs.astype(BF16), spots, (((1,), (1,)), ((), ())), preferred_element_type=F32
    )
    image = image[:16] + image[16:]
    sa[...] = image
    ga[0] = image
    send(sa.at[pl.ds(0, 10)], ga.at[:, pl.ds(0, 10)], y_of, far_y, sem_a)

    for c in (all_y, all_w, all_q, all_h):
        c.wait_send()
    all_a.wait()

def place(adv, ga, pick, adv_out, snap_out, snap, sems):
    first = pltpu.make_async_copy(adv, adv_out, sems.at[0])
    first.start()
    hi, lo = split(ga[...].reshape(ga.shape[0] * 16, 128))
    snap[...] = mm(pick[...], hi) + mm(pick[...], lo)
    second = pltpu.make_async_copy(snap, snap_out, sems.at[1])
    second.start()
    first.wait()
    second.wait()


def shards(ngx, ngy, state, counts, aggregator):
    first, second, ranks, cmat = tables()
    vm = pltpu.VMEM
    dma = pltpu.SemaphoreType.DMA
    vmem = pl.BlockSpec(memory_space=pltpu.VMEM)
    adv, images, pick = pl.pallas_call(
        functools.partial(kernel, ngx, ngy),
        out_shape=(
            vm((5, 8, 8, 128), F32),
            vm((ngy, 16, 128), F32),
            vm((ngy * 5, ngy * 16), BF16),
        ),
        in_specs=[pl.BlockSpec(memory_space=pltpu.HBM)] * 7,
        out_specs=(vmem, vmem, vmem),
        scratch_shapes=[
            vm(state.shape, F32),
            vm(counts.shape, jnp.int32),
            vm((1, 1), jnp.int32),
            vm(first.shape, BF16),
            vm(second.shape, BF16),
            vm(ranks.shape, jnp.int32),
            vm(cmat.shape, F32),
            dma((9,)),
            vm((5, 16, 8, 128), F32),
            vm((5, 12, 8, 128), F32),
            vm((5, 12, 8, 128), F32),
            vm((5, 12, 8, 128), F32),
            vm((5, 12, 8, 128), F32),
            vm((5, 12, 8, 128), F32),
            vm((5, 12, 8, 128), F32),
            vm((5, 8, 8, 128), F32),
            vm((5, 8, 8, 128), F32),
            vm((2, 5, 6, 8, 128), F32),
            vm((2, 5, 6, 8, 128), F32),
            vm((5, 8, 128), F32),
            vm((6, 5, 8, 128), F32),
            vm((2, 5, 2, 8, 128), F32),
            vm((2, 1, 128), F32),
            vm((ngy, 1, 128), F32),
            vm((ngx, 1, 128), F32),
            vm((ngy, 128), F32),
            vm((16, 128), F32),
            vm((2, 5, 7, 8, 128), F32),
            vm((4, 5, 8, 128), F32),
            dma((2,)), dma((2,)), dma((2,)), dma((2,)), dma((2,)),
        ],
        compiler_params=pltpu.CompilerParams(collective_id=0, has_side_effects=True),
        name="step",
    )(state, counts, aggregator.reshape(1, 1), first, second, ranks, cmat)
    hbm = pl.BlockSpec(memory_space=pltpu.HBM)
    adv, snap = pl.pallas_call(
        place,
        out_shape=(jax.ShapeDtypeStruct(adv.shape, F32), jax.ShapeDtypeStruct((ngy * 5, 128), F32)),
        in_specs=[vmem] * 3,
        out_specs=(hbm, hbm),
        scratch_shapes=[vm((ngy * 5, 128), F32), dma((2,))],
        compiler_params=pltpu.CompilerParams(vmem_limit_bytes=1 << 20),
        name="place",
    )(adv, images, pick)
    return adv, snap.reshape(1, 1, ngy * 640)


def solution(mesh):
    ngx, ngy = mesh.shape["gx"], mesh.shape["gy"]
    placed = (P(None, None, "gx", "gy"), P(None, None, "gx", "gy"), P("gx"))
    return jax.shard_map(
        functools.partial(shards, ngx, ngy),
        mesh=mesh,
        in_specs=placed,
        out_specs=(P(None, None, "gx", "gy"), P("gx", "gy", None)),
        check_vma=False,
    )
```
